32 devices in a mesh: dp: 8 (over z, core), expert: 4 (over y, x).
Axes of the slice: x: 2, y: 2, z: 4, core: 2. Of those that a mesh axis runs over, the one named last changes fastest.
Arguments:
- token_ids: int32 [32, 512], P('dp'), may hold values from 0 to 31999
- segments: int32 [32, 512], P(('dp', 'expert')), may hold values from 0 to 3, never falling along the last dimension, each value on 1 to 320 neighbouring positions
- routes: int32 [32, 512, 2], P('dp'), may hold values from 0 to 7, all different within a row; in each aligned block of 512 rows (0 to 511, 512 to 1023, ..., all dimensions but the last counted through in order) at most 192 rows name the same one
- positions: int32 [2048], P(('dp', 'expert')), may hold values from 0 to 511
- targets: int32 [2048], P('dp'), may hold values from 0 to 31999
- teacher_ids: int32 [2048, 64], P('dp'), may hold values from 0 to 31999
- teacher_probs: float32 [2048, 64], P('dp'), as said below
- attention: float32 [4, 768, 768], P(None, 'dp'), may hold values from -0.21875 to 0.21875
- attention_moment: float32 [4, 768, 768], P(None, 'dp'), may hold values from -0.013671875 to 0.013671875
- attention_average: float32 [4, 768, 768], P(None, 'dp'), may hold values from -0.21875 to 0.21875
- expert_in: float32 [8, 768, 3072], P('expert', 'dp'), may hold values from -0.21875 to 0.21875
- expert_in_moment: float32 [8, 768, 3072], P('expert', 'dp'), may hold values from -0.0024414062 to 0.0024414062
- expert_in_average: float32 [8, 768, 3072], P('expert', 'dp'), may hold values from -0.21875 to 0.21875
- expert_out: float32 [8, 3072, 768], P('expert', 'dp'), may hold values from -0.02734375 to 0.02734375
- expert_out_moment: float32 [8, 3072, 768], P('expert', 'dp'), may hold values from -0.013671875 to 0.013671875
- expert_out_average: float32 [8, 3072, 768], P('expert', 'dp'), may hold values from -0.02734375 to 0.02734375
- embedding: float32 [32000, 768], P('expert', 'dp'), may hold values from -0.4375 to 0.4375
- embedding_moment: float32 [32000, 768], P('expert', 'dp'), may hold values from -0.0012207031 to 0.0012207031
- embedding_average: float32 [32000, 768], P('expert', 'dp'), may hold values from -0.4375 to 0.4375
- small_params: float32 [11, 768], P(None, 'dp')
- small_moment: float32 [11, 768], P(None, 'dp'), may hold values from -0.0390625 to 0.0390625
- small_average: float32 [11, 768], P(None, 'dp'), may hold values from -3 to 3
Outputs:
- loss_value: float32 [], replicated
- attention_next: float32 [4, 768, 768], P(None, 'dp')
- attention_moment_next: float32 [4, 768, 768], P(None, 'dp')
- attention_average_next: float32 [4, 768, 768], P(None, 'dp')
- attention_copy: bfloat16 [4, 768, 768], P(None, 'dp')
- expert_in_next: float32 [8, 768, 3072], P('expert', 'dp')
- expert_in_moment_next: float32 [8, 768, 3072], P('expert', 'dp')
- expert_in_average_next: float32 [8, 768, 3072], P('expert', 'dp')
- expert_in_copy: bfloat16 [8, 768, 3072], P('expert', 'dp')
- expert_out_next: float32 [8, 3072, 768], P('expert', 'dp')
- expert_out_moment_next: float32 [8, 3072, 768], P('expert', 'dp')
- expert_out_average_next: float32 [8, 3072, 768], P('expert', 'dp')
- expert_out_copy: bfloat16 [8, 3072, 768], P('expert', 'dp')
- embedding_next: float32 [32000, 768], P('expert', 'dp')
- embedding_moment_next: float32 [32000, 768], P('expert', 'dp')
- embedding_average_next: float32 [32000, 768], P('expert', 'dp')
- embedding_copy: bfloat16 [32000, 768], P('expert', 'dp')
- small_next: float32 [11, 768], P(None, 'dp')
- small_moment_next: float32 [11, 768], P(None, 'dp')
- small_average_next: float32 [11, 768], P(None, 'dp')
- small_copy: bfloat16 [11, 768], P(None, 'dp')
The draws below stay inside these ranges and needn't reach their ends.
Inputs may be any that keep to these rules, and one draw needn't show every extreme that they name: `routes`: each row names 2 different experts; in the rows of one device (aligned blocks of 512 rows) no expert is named by more than 192 rows, a bound that some block reaches. `segments`: never falling along a sequence. `teacher_probs`: Positive; each row sums to one.
All inputs are finite; a program needn't handle non-finite values.
Results may differ from the reference program's by a relative error of at most 0.01195.
The reference program's roundings to bfloat16 on the way count: a program that leaves them out, or rounds other values in their place, can miss the bound.
Values may be sent and summed in bfloat16 or wider, within the bound.
No kernel may reach another device: no remote copies, remote signals or barrier semaphores. Data moves between devices by JAX's collectives and lax.ppermute only.
A program may use at most 320 MiB of HBM per device.

```python
import math
import jax
import jax.numpy as jnp
import numpy as np
from jax import lax

D = 768
HEADS = 12
HEAD = 64
FF = 3072
VOCAB = 32000
TOP = 2
SEQ = 512
LOSS_DEV = 64
TEACH = 64
STEP = 7
EXPERTS = 8
TOK_DEV = 512
SEQUENCES = 32
TOKENS = 16384
LOSS_ALL = 2048
CAP = 192


def draw_teacher_probs(key, part):
    scores = 1.5 * jax.random.normal(key, (LOSS_ALL, TEACH), jnp.float32)
    return jax.nn.softmax(scores, axis=1)


def draw_small_params(key, part):
    first_key, second_key = jax.random.split(key)
    gain_rows = 1.0 + 0.15 * jax.random.normal(first_key, (3, D), jnp.float32)
    router = 0.7 / D ** 0.5 * jax.random.normal(second_key, (EXPERTS, D), jnp.float32)
    return jnp.concatenate([gain_rows, router], axis=0)


def touch_ends(values, own_key, least, high):
    longest = values.shape.index(max(values.shape))
    spots = []
    for shift in (0, 1):
        where = [jax.random.randint(jax.random.fold_in(own_key, axis), (), 0, length) for axis, length in enumerate(values.shape)]
        where[longest] = (where[longest] + shift) % values.shape[longest]
        spots.append(tuple(where))
    return values.at[spots[0]].set(least).at[spots[1]].set(high)


def shard_levels(stream_key, shape, cuts, low, top_value):
    def one(axis_at, parts):
        steps = jax.random.uniform(jax.random.fold_in(jax.random.fold_in(stream_key, 6), axis_at), (parts,), jnp.float32, low / len(cuts), top_value / len(cuts))
        return jnp.repeat(jnp.exp(steps), shape[axis_at] // parts).reshape((-1,) + (1,) * (len(shape) - axis_at - 1))

    loudness = one(*cuts[0])
    for cut in cuts[1:]:
        loudness = loudness * one(*cut)
    return loudness


def rank_bounds(number_of, lean):
    portions = [(1 << 20) // math.isqrt(rank ** lean) + 1 for rank in range(1, number_of + 1)]
    spread = 1 + sum(portions) // (1 << 30)
    return np.cumsum(np.array([max(1, weight // spread) for weight in portions]))


def ranked(stream_key, shape, number_of, lean):
    listing = rank_bounds(number_of, lean)
    pick = jax.random.randint(jax.random.fold_in(stream_key, 1), shape, 0, int(listing[number_of - 1]))
    grade = jnp.searchsorted(jnp.asarray(listing, jnp.int32), pick, side="right")
    return jax.random.permutation(jax.random.fold_in(stream_key, 2), number_of)[grade].astype(jnp.int32)


def split_up(number_of, total, reach, slope):
    loads = [(1 << 20) // math.isqrt(grade ** slope) + 1 for grade in range(2, number_of + 1)]
    spare, holding = total - reach - (number_of - 1), [1] * (number_of - 1)
    while spare > 0:
        candidates = [i for i in range(number_of - 1) if holding[i] < reach]
        mass, remaining = sum([loads[i] for i in candidates]), spare
        for i in candidates:
            addition = min(reach - holding[i], max(1, remaining * loads[i] // mass), spare)
            holding[i] = holding[i] + addition
            spare = spare - addition
    return np.array([reach] + holding)


def uneven(stream_key, count, total, most, skew):
    if count == 2:
        one = jax.random.randint(stream_key, (), max(1, total - most), min(most, total - 1) + 1)
        return jnp.stack([one, total - one])
    tallies = jnp.asarray(split_up(count, total, most, skew), jnp.int32)
    pairs = (count - 1) // 2
    donor, receiver = tallies[1:1 + 2 * pairs:2], tallies[2:2 + 2 * pairs:2]
    slack = jnp.minimum(donor - 1, most - receiver)
    moved = jax.random.randint(jax.random.fold_in(stream_key, 1), (pairs,), 0, 1 << 20) % (slack + 1)
    tallies = tallies.at[1:1 + 2 * pairs:2].set(donor - moved).at[2:2 + 2 * pairs:2].set(receiver + moved)
    return tallies[jax.random.permutation(jax.random.fold_in(stream_key, 2), count)]


def deal_out(own_key, own, number, rows, amount, top, limit, skew):
    order = jax.random.permutation(own_key, amount)
    heavy_load, common = shares(amount, rows * top, limit, skew, True), shares(amount, rows * top, limit, skew, False)
    places = jnp.arange(amount)

    def named(lengths, rotation):
        used = int((lengths > 0).sum())
        fixed = max(1, used // 4)
        shifted = fixed + (places - fixed + rotation * (used - fixed)) % max(1, amount - fixed)
        return jnp.zeros((amount,), jnp.int32).at[order[jnp.where(places < fixed, places, shifted)]].set(jnp.asarray(lengths, jnp.int32))

    lengths = jnp.where(number % 4 == 0, named(heavy_load, number // 4), named(common, number - number // 4 - 1))
    mixed = jax.random.permutation(jax.random.fold_in(own, 3), amount)
    source_of, sink = mixed[0:amount // 2 * 2:2], mixed[1:amount // 2 * 2:2]
    room = jnp.minimum(lengths[source_of] - 1, limit - lengths[sink]) // 2
    room = jnp.where((source_of == order[0]) | (sink == order[0]) | (lengths[sink] == 0), 0, jnp.maximum(room, 0))
    shifted = jax.random.randint(jax.random.fold_in(own, 4), (amount // 2,), 0, 1 << 20) % (room + 1)
    lengths = lengths.at[source_of].add(-shifted).at[sink].add(shifted)
    members = jnp.searchsorted(jnp.cumsum(lengths), jnp.arange(rows * top), side="right").astype(jnp.int32)
    table = members.reshape(top, rows).T
    table = table[jax.random.permutation(jax.random.fold_in(own, 1), rows)]
    rotation = jax.random.randint(jax.random.fold_in(own, 2), (rows, 1), 0, top)
    return jnp.take_along_axis(table, (jnp.arange(top)[None, :] + rotation) % top, axis=1)


def shares(number_of, total, bound, skew, full):
    portions = [(1 << 20) // math.isqrt(rank ** skew) + 1 for rank in range(1, number_of + 1)]
    largest = bound if full else min(bound, max(-(-total // number_of), total * portions[0] // sum(portions)))
    least = 1 if total - largest >= number_of - 1 else 0
    holding, spare = [largest] + [least] * (number_of - 1), total - largest - least * (number_of - 1)
    while spare > 0:
        free = [i for i in range(1, number_of) if holding[i] < largest] or [i for i in range(1, number_of) if holding[i] < bound]
        whole, left = sum([portions[i] for i in free]), spare
        for i in free:
            addition = min(bound - holding[i], max(1, left * portions[i] // whole), spare)
            holding[i] = holding[i] + addition
            spare = spare - addition
    return np.array(holding)


def bell_draw(stream_key, extent, spread, limit, cuts=(), held_as=jnp.bfloat16):
    entries = jax.random.normal(stream_key, extent, jnp.float32) * spread
    if len(cuts) > 0:
        entries = shard_levels(stream_key, extent, cuts, -0.22, 0.18) * entries
    return jnp.clip(entries, min=-limit, max=limit).astype(held_as)


def setup_inputs(seed: int = 0) -> dict:
    splits = jax.random.split(jax.random.key(seed), 23)
    token_ids = touch_ends(ranked(splits[0], (SEQUENCES, SEQ), VOCAB, 2), jax.random.fold_in(splits[0], 3), 0, VOCAB - 1).astype(jnp.int32)
    segments = jax.vmap(lambda own: jnp.searchsorted(jnp.cumsum(uneven(own, 4, SEQ, SEQ * 5 // 8, 2)), jnp.arange(SEQ), side="right"))(jax.random.split(splits[1], SEQUENCES)).reshape((SEQUENCES, SEQ)).astype(jnp.int32)
    routes_keys = jax.random.split(jax.random.fold_in(splits[2], 1), SEQUENCES * SEQ // TOK_DEV)
    routes_turns = jax.random.permutation(jax.random.fold_in(splits[2], 3), SEQUENCES * SEQ // TOK_DEV)
    routes = jax.vmap(lambda own, number: deal_out(jax.random.fold_in(splits[2], 2), own, number, TOK_DEV, EXPERTS, TOP, CAP, 1))(routes_keys, routes_turns).reshape((SEQUENCES, SEQ, TOP))
    positions = touch_ends(jax.random.randint(splits[3], (LOSS_ALL,), 0, TOK_DEV), jax.random.fold_in(splits[3], 1), 0, TOK_DEV - 1).astype(jnp.int32)
    targets = touch_ends(ranked(splits[4], (LOSS_ALL,), VOCAB, 2), jax.random.fold_in(splits[4], 3), 0, VOCAB - 1).astype(jnp.int32)
    teacher_ids = touch_ends(ranked(splits[5], (LOSS_ALL, TEACH), VOCAB, 2), jax.random.fold_in(splits[5], 3), 0, VOCAB - 1).astype(jnp.int32)
    teacher_probs = draw_teacher_probs(jax.random.fold_in(splits[22], 71), 0)
    attention = bell_draw(splits[7], (4, D, D), D ** -0.5, 0.21875, ((1, 8),), jnp.float32)
    attention_moment = bell_draw(splits[8], (4, D, D), (0.1 / LOSS_ALL ** 0.5), 0.013671875, ((1, 8),), jnp.float32)
    attention_average = bell_draw(splits[9], (4, D, D), D ** -0.5, 0.21875, ((1, 8),), jnp.float32)
    expert_in = bell_draw(splits[10], (EXPERTS, D, FF), D ** -0.5, 0.21875, ((0, 4), (1, 8)), jnp.float32)
    expert_in_moment = bell_draw(splits[11], (EXPERTS, D, FF), (0.02 / LOSS_ALL ** 0.5), 0.0024414062, ((0, 4), (1, 8)), jnp.float32)
    expert_in_average = bell_draw(splits[12], (EXPERTS, D, FF), D ** -0.5, 0.21875, ((0, 4), (1, 8)), jnp.float32)
    expert_out = bell_draw(splits[13], (EXPERTS, FF, D), (FF * 16) ** -0.5, 0.02734375, ((0, 4), (1, 8)), jnp.float32)
    expert_out_moment = bell_draw(splits[14], (EXPERTS, FF, D), (0.1 / LOSS_ALL ** 0.5), 0.013671875, ((0, 4), (1, 8)), jnp.float32)
    expert_out_average = bell_draw(splits[15], (EXPERTS, FF, D), (FF * 16) ** -0.5, 0.02734375, ((0, 4), (1, 8)), jnp.float32)
    embedding = bell_draw(splits[16], (VOCAB, D), (2.0 / D ** 0.5), 0.4375, ((0, 4), (1, 8)), jnp.float32)
    embedding_moment = bell_draw(splits[17], (VOCAB, D), (0.01 / LOSS_ALL ** 0.5), 0.0012207031, ((0, 4), (1, 8)), jnp.float32)
    embedding_average = bell_draw(splits[18], (VOCAB, D), (2.0 / D ** 0.5), 0.4375, ((0, 4), (1, 8)), jnp.float32)
    small_params = draw_small_params(jax.random.fold_in(splits[22], 71), 0)
    small_moment = bell_draw(splits[20], (3 + EXPERTS, D), (0.3 / LOSS_ALL ** 0.5), 0.0390625, ((1, 8),), jnp.float32)
    small_average = bell_draw(splits[21], (3 + EXPERTS, D), 0.5, 3.0, ((1, 8),), jnp.float32)
    return dict(token_ids=token_ids, segments=segments, routes=routes, positions=positions, targets=targets, teacher_ids=teacher_ids, teacher_probs=teacher_probs, attention=attention, attention_moment=attention_moment, attention_average=attention_average, expert_in=expert_in, expert_in_moment=expert_in_moment, expert_in_average=expert_in_average, expert_out=expert_out, expert_out_moment=expert_out_moment, expert_out_average=expert_out_average, embedding=embedding, embedding_moment=embedding_moment, embedding_average=embedding_average, small_params=small_params, small_moment=small_moment, small_average=small_average)


@jax.custom_vjp
def low(v):
    return lax.optimization_barrier(v.astype(jnp.bfloat16)).astype(jnp.float32)

@jax.custom_vjp
def low_back(v):
    return v

def low_keep(v):
    return (low(v), None)

def low_pass(kept, grad):
    return (grad,)

def back_keep(v):
    return (v, None)

def back_low(kept, grad):
    return (low(grad),)
low.defvjp(low_keep, low_pass)
low_back.defvjp(back_keep, back_low)
PRECISE = lax.Precision.HIGHEST
EPSILON = 1e-06
MOMENTUM = 0.9
RATE_TABLE = (0.1, 0.3, 0.01, 0.05, 0.05)
MASKED_SCORE = -1e+30

def normalize(stream):
    return stream * lax.rsqrt(lax.optimization_barrier(jnp.mean(stream * stream, axis=-1, keepdims=True)) + EPSILON)

def softmax_rows(scores):
    highest = lax.optimization_barrier(jnp.max(scores, axis=-1, keepdims=True))
    powers = jnp.exp(scores - highest)
    return powers / lax.optimization_barrier(jnp.sum(powers, axis=-1, keepdims=True))

def slot_table(block_routes):
    flat = block_routes.reshape(-1)
    hits = (flat[:, None] == jnp.arange(EXPERTS, dtype=jnp.int32)[None, :]).astype(jnp.int32)
    before = jnp.cumsum(hits, axis=0) - hits
    return (flat, lax.optimization_barrier(jnp.sum(before * hits, axis=1)).astype(jnp.int32))

def attend(stream, seg_ids, matrices, gain):
    normal_in = low(normalize(stream) * gain)
    query = low(low_back(jnp.dot(normal_in, matrices[0], precision=PRECISE))).reshape(SEQ, HEADS, HEAD)
    keys = low(low_back(jnp.dot(normal_in, matrices[1], precision=PRECISE))).reshape(SEQ, HEADS, HEAD)
    values = low(low_back(jnp.dot(normal_in, matrices[2], precision=PRECISE))).reshape(SEQ, HEADS, HEAD)
    scores = low_back(jnp.einsum('qhd,khd->hqk', query, keys, precision=PRECISE) * HEAD ** (-0.5))
    places = jnp.arange(SEQ)
    allowed = (places[None, :] <= places[:, None]) & (seg_ids[None, :] == seg_ids[:, None])
    soft = softmax_rows(jnp.where(allowed[None], scores, MASKED_SCORE))
    mixed = jnp.einsum('hqk,khd->qhd', low(soft), values, precision=PRECISE).reshape(SEQ, D)
    mixed = low(low_back(mixed))
    return low_back(jnp.dot(mixed, matrices[3], precision=PRECISE))

def forward(attention, expert_in, expert_out, embedding, small_params, token_ids, segments, routes, positions, targets, teacher_ids, teacher_probs):
    matrices = low(attention)
    in_low = low(expert_in)
    out_low = low(expert_out)
    table = low(embedding)
    small_low = low(small_params)
    router = small_low[3:]
    stream = low_back(jnp.take(table, token_ids.reshape(-1), axis=0))

    def one_sequence(pair):
        return attend(pair[0], pair[1], matrices, small_low[0])
    attn_out = lax.map(jax.checkpoint(one_sequence), (stream.reshape(SEQUENCES, SEQ, D), segments))
    hidden_one = stream + attn_out.reshape(TOKENS, D)
    moe_in = low(normalize(hidden_one) * small_low[1])
    router_logits = jnp.dot(moe_in, router.T, precision=PRECISE)
    flat_routes = routes.reshape(TOKENS, TOP)
    gating = softmax_rows(jnp.take_along_axis(router_logits, flat_routes, axis=1))
    block_count = TOKENS // TOK_DEV
    flat, slots = jax.vmap(slot_table)(flat_routes.reshape(block_count, TOK_DEV, TOP))
    column = jnp.arange(block_count, dtype=jnp.int32)[:, None] * CAP + slots
    token_rows = (jnp.arange(TOKENS * TOP, dtype=jnp.int32) // TOP).reshape(block_count, TOK_DEV * TOP)
    index_table = jnp.full((EXPERTS, block_count * CAP), TOKENS, jnp.int32)
    index_table = index_table.at[flat.reshape(-1), column.reshape(-1)].set(token_rows.reshape(-1))
    padded = jnp.concatenate([moe_in, jnp.zeros((1, D), jnp.float32)], axis=0)

    def run_expert(triple):
        rows = jnp.take(padded, triple[0], axis=0)
        hidden = low_back(jnp.dot(rows, triple[1], precision=PRECISE))
        acted = low(jax.nn.gelu(hidden, approximate=True))
        return low(low_back(jnp.dot(acted, triple[2], precision=PRECISE)))
    results = lax.map(jax.checkpoint(run_expert), (index_table, in_low, out_low))
    picked = results[flat.reshape(-1), column.reshape(-1)].reshape(TOKENS, TOP, D)
    hidden_two = hidden_one + lax.optimization_barrier(jnp.sum(gating[:, :, None] * picked, axis=1))
    final = low(normalize(hidden_two) * small_low[2])
    rows_at = jnp.arange(LOSS_ALL, dtype=jnp.int32) // LOSS_DEV * TOK_DEV + positions
    final_rows = jnp.take(final, rows_at, axis=0)
    logits = low_back(jnp.dot(final_rows, table.T, precision=PRECISE))
    highest = lax.optimization_barrier(jnp.max(logits, axis=1))
    log_total = highest + jnp.log(lax.optimization_barrier(jnp.sum(jnp.exp(logits - highest[:, None]), axis=1)))
    target_logit = jnp.take_along_axis(logits, targets[:, None], axis=1)[:, 0]
    taught = lax.optimization_barrier(jnp.sum(teacher_probs * jnp.take_along_axis(logits, teacher_ids, axis=1), axis=1))
    entropy = lax.optimization_barrier(jnp.sum(teacher_probs * jnp.log(teacher_probs), axis=1))
    return jnp.sum(2.0 * log_total - target_logit - taught + entropy) / LOSS_ALL

def nesterov_update(master, moment, average, grad, rate):
    moment_next = MOMENTUM * moment + grad
    master_next = master - rate * (grad + MOMENTUM * moment_next)
    average_next = average + (master_next - average) / (STEP + 1)
    return (master_next, moment_next, average_next, master_next.astype(jnp.bfloat16))

def reference(token_ids, segments, routes, positions, targets, teacher_ids, teacher_probs, attention, attention_moment, attention_average, expert_in, expert_in_moment, expert_in_average, expert_out, expert_out_moment, expert_out_average, embedding, embedding_moment, embedding_average, small_params, small_moment, small_average):

    def loss_of(attention_all, in_all, out_all, table_all, small_all):
        return forward(attention_all, in_all, out_all, table_all, small_all, token_ids, segments, routes, positions, targets, teacher_ids, teacher_probs)
    loss_value, pull_back = jax.vjp(loss_of, attention, expert_in, expert_out, embedding, small_params)
    grads = pull_back(jnp.ones_like(loss_value))
    base = math.sqrt(LOSS_ALL)
    first = nesterov_update(attention, attention_moment, attention_average, grads[0], RATE_TABLE[0] * base)
    second = nesterov_update(expert_in, expert_in_moment, expert_in_average, grads[1], RATE_TABLE[1] * base)
    third = nesterov_update(expert_out, expert_out_moment, expert_out_average, grads[2], RATE_TABLE[2] * base)
    fourth = nesterov_update(embedding, embedding_moment, embedding_average, grads[3], RATE_TABLE[3] * base)
    fifth = nesterov_update(small_params, small_moment, small_average, grads[4], RATE_TABLE[4] * base)
    return (loss_value, first[0], first[1], first[2], first[3], second[0], second[1], second[2], second[3], third[0], third[1], third[2], third[3], fourth[0], fourth[1], fourth[2], fourth[3], fifth[0], fifth[1], fifth[2], fifth[3])
```

```python
import math

import jax
import jax.numpy as jnp
from jax import lax
from jax.sharding import PartitionSpec as P

HEAD = 64
TOP = 2
STEP = 7


EPSILON = 1e-06
MOMENTUM = 0.9
RATE_TABLE = (0.1, 0.3, 0.01, 0.05, 0.05)
MASKED_SCORE = -1e30


def combined_all(value, axis, join):
    pieces = jax.tree.map(lambda part: lax.all_gather(part, axis), value)
    head = jax.tree.map(lambda part: part[0], pieces)
    tail = jax.tree.map(lambda part: part[1:], pieces)
    total, _ = lax.scan(lambda total, share: (join(total, share), None), head, tail)
    return total


def normal_parts(stream):
    factor = lax.rsqrt(jnp.mean(stream * stream, axis=-1, keepdims=True) + EPSILON)
    return (stream * factor, factor)


def norm_backward(normal, factor, gain, grad):
    gain_grad = jnp.sum(grad * normal, axis=0)
    normal_grad = grad * gain
    inner = jnp.mean(normal_grad * normal, axis=-1, keepdims=True)
    return (factor * (normal_grad - normal * inner), gain_grad)


def slot_table(block_routes, experts):
    flat = block_routes.reshape(-1)
    hits = (flat[:, None] == jnp.arange(experts, dtype=jnp.int32)[None, :]).astype(jnp.int32)
    place = jnp.arange(flat.shape[0], dtype=jnp.int32)
    earlier = (place[None, :] < place[:, None]).astype(jnp.bfloat16)
    before = jnp.dot(earlier, hits.astype(jnp.bfloat16), preferred_element_type=jnp.float32)
    return (flat, jnp.sum(before.astype(jnp.int32) * hits, axis=1))


def block_scores(query, keys, seg_ids, block_index, length, block_rows, scaling):
    start = block_index * block_rows
    first_row = start // length * length
    scores = jnp.einsum("qhd,khd->hqk", query, keys, preferred_element_type=jnp.float32) * scaling
    query_place = start - first_row + jnp.arange(block_rows)
    allowed = (jnp.arange(length)[None, :] <= query_place[:, None]) & (
        seg_ids[None, :] == seg_ids[:, None]
    )
    return (jnp.where(allowed[None], scores, MASKED_SCORE), query, keys, first_row)


def combine_stats(earlier, later):
    highest = jnp.maximum(earlier[0], later[0])
    totals = earlier[1] * jnp.exp(earlier[0] - highest) + later[1] * jnp.exp(later[0] - highest)
    return (highest, totals, earlier[2] + later[2])


def nesterov_update(master, moment, average, grad, rate):
    moment_next = MOMENTUM * moment + grad
    master_next = master - rate * (grad + MOMENTUM * moment_next)
    average_next = average + (master_next - average) / (STEP + 1)
    return (master_next, moment_next, average_next, master_next.astype(jnp.bfloat16))


def shards(
    token_ids,
    segments,
    routes,
    positions,
    targets,
    teacher_ids,
    teacher_probs,
    attention,
    attention_moment,
    attention_average,
    expert_in,
    expert_in_moment,
    expert_in_average,
    expert_out,
    expert_out_moment,
    expert_out_average,
    embedding,
    embedding_moment,
    embedding_average,
    small_params,
    small_moment,
    small_average,
):
    members = lax.axis_size("expert")
    replicas = lax.axis_size("dp")
    my_index = lax.axis_index("expert")
    length = segments.shape[1]
    local_rows = segments.shape[0] * length
    width = attention.shape[2]
    head_count = width // HEAD
    local_experts = expert_in.shape[0]
    experts = local_experts * members
    vocab_rows = embedding.shape[0]
    capacity = max(2, 3 * local_rows * TOP // (2 * experts))
    loss_local = positions.shape[0]
    loss_count = loss_local * members * replicas
    block_rows = min(512, length)
    block_count = local_rows // block_rows
    scaling = HEAD ** (-0.5)
    highest_precision = lax.Precision.HIGHEST
    group_count = members * local_rows
    lookup_rows = math.gcd(group_count, 2048)
    vocab_iota = jnp.arange(vocab_rows, dtype=jnp.int32)
    dense_low, small_low = (
        lax.all_gather(attention.astype(jnp.bfloat16), "dp", axis=1, tiled=True),
        lax.all_gather(small_params.astype(jnp.bfloat16), "dp", axis=1, tiled=True),
    )
    in_low, out_low, table_low = (
        lax.all_gather(expert_in.astype(jnp.bfloat16), "dp", axis=1, tiled=True),
        lax.all_gather(expert_out.astype(jnp.bfloat16), "dp", axis=1, tiled=True),
        lax.all_gather(embedding.astype(jnp.bfloat16), "dp", axis=1, tiled=True),
    )
    gain_rows = small_low[:3].astype(jnp.float32)
    router = small_low[3:].astype(jnp.float32)
    group_ids = token_ids.reshape(-1)
    group_routes = routes.reshape(members * local_rows, TOP)
    own_routes = lax.dynamic_slice_in_dim(group_routes, my_index * local_rows, local_rows, 0)
    local_ids = group_ids - my_index * vocab_rows
    id_blocks = local_ids.reshape(group_count // lookup_rows, lookup_rows)

    def lookup_block(ids_block):
        selector = (ids_block[:, None] == vocab_iota[None, :]).astype(jnp.bfloat16)
        return jnp.dot(selector, table_low, preferred_element_type=jnp.float32).astype(jnp.bfloat16)

    partial_value = lax.map(lookup_block, id_blocks).reshape(group_count, width)
    stream = lax.psum_scatter(partial_value, "expert", scatter_dimension=0, tiled=True).astype(
        jnp.float32
    )
    normal_one, factor_one = normal_parts(stream)
    attn_in = (normal_one * gain_rows[0]).astype(jnp.bfloat16)
    projected = jnp.einsum(
        "td,jde->jte", attn_in, dense_low[:3], preferred_element_type=jnp.float32
    ).astype(jnp.bfloat16)
    query = projected[0].reshape(local_rows, head_count, HEAD)
    keys = projected[1].reshape(local_rows, head_count, HEAD)
    values = projected[2].reshape(local_rows, head_count, HEAD)
    seg_ids = segments.reshape(-1)

    def forward_block(block_index):
        scores, query_block, key_block, first_row = block_scores(
            query, keys, seg_ids, block_index, length, block_rows, scaling
        )
        highest = jnp.max(scores, axis=-1, keepdims=True)
        powers = jnp.exp(scores - highest)
        totals = jnp.sum(powers, axis=-1, keepdims=True)
        mixed_block = jnp.einsum(
            "hqk,khd->qhd",
            (powers / totals).astype(jnp.bfloat16),
            values,
            preferred_element_type=jnp.float32,
        )
        return (mixed_block, (highest + jnp.log(totals))[..., 0])

    mixed_blocks, log_totals = lax.map(forward_block, jnp.arange(block_count))
    mixed = mixed_blocks.reshape(local_rows, width).astype(jnp.bfloat16)
    hidden_one = stream + jnp.dot(mixed, dense_low[3], preferred_element_type=jnp.float32)
    normal_two, factor_two = normal_parts(hidden_one)
    moe_in = (normal_two * gain_rows[1]).astype(jnp.bfloat16)
    moe_float = moe_in.astype(jnp.float32)
    router_logits = jnp.dot(moe_float, router.T, precision=highest_precision)
    chosen = jnp.take_along_axis(router_logits, own_routes, axis=1)
    gating = jnp.exp(chosen - jnp.max(chosen, axis=1, keepdims=True))
    gating = gating / jnp.sum(gating, axis=1, keepdims=True)
    flat_routes, slots = slot_table(own_routes, experts)
    landing = flat_routes * capacity + slots
    token_of = jnp.arange(local_rows * TOP) // TOP
    everyone = lax.all_gather(moe_in, "expert", axis=0, tiled=True)
    all_flat, all_slots = jax.vmap(lambda block_routes: slot_table(block_routes, experts))(
        group_routes.reshape(members, local_rows, TOP)
    )
    owned = all_flat - my_index * local_experts
    source = jnp.arange(members)[:, None]
    spot = owned * (members * capacity) + source * capacity + all_slots
    spot = jnp.where(
        (owned >= 0) & (owned < local_experts), spot, local_experts * members * capacity
    )
    source_rows = source * local_rows + token_of[None, :]
    arrived = (
        jnp.zeros((local_experts * members * capacity, width), jnp.bfloat16)
        .at[spot.reshape(-1)]
        .set(jnp.take(everyone, source_rows.reshape(-1), axis=0), mode="drop")
    )
    arrived = arrived.reshape(local_experts, members * capacity, width)
    expert_hidden = jnp.einsum("ecd,edf->ecf", arrived, in_low, preferred_element_type=jnp.float32)
    activated = jax.nn.gelu(expert_hidden, approximate=True).astype(jnp.bfloat16)
    expert_result = jnp.einsum(
        "ecf,efd->ecd", activated, out_low, preferred_element_type=jnp.float32
    ).astype(jnp.bfloat16)
    returned = lax.all_to_all(
        expert_result.reshape(local_experts, members, capacity, width),
        "expert",
        split_axis=1,
        concat_axis=0,
        tiled=True,
    )
    returned = returned.reshape(experts * capacity, width)
    picked = jnp.take(returned, landing, axis=0).reshape(local_rows, TOP, width).astype(jnp.float32)
    hidden_two = hidden_one + jnp.sum(gating[:, :, None] * picked, axis=1)
    normal_three, factor_three = normal_parts(hidden_two)
    final = (normal_three * gain_rows[2]).astype(jnp.bfloat16)
    group_final = lax.all_gather(jnp.take(final, positions, axis=0), "expert", axis=0, tiled=True)
    logits = jnp.einsum("gd,vd->gv", group_final, table_low, preferred_element_type=jnp.float32)
    target_local = targets - my_index * vocab_rows
    teacher_local = teacher_ids - my_index * vocab_rows
    target_inside = (target_local >= 0) & (target_local < vocab_rows)
    teacher_inside = (teacher_local >= 0) & (teacher_local < vocab_rows)
    target_logit = jnp.take_along_axis(
        logits, jnp.clip(target_local, 0, vocab_rows - 1)[:, None], axis=1
    )[:, 0]
    teacher_logit = jnp.take_along_axis(logits, jnp.clip(teacher_local, 0, vocab_rows - 1), axis=1)
    taught = jnp.where(target_inside, target_logit, 0.0) + jnp.sum(
        jnp.where(teacher_inside, teacher_probs * teacher_logit, 0.0), axis=1
    )
    local_max = jnp.max(logits, axis=1)
    local_total = jnp.sum(jnp.exp(logits - local_max[:, None]), axis=1)
    highest, totals, picked_sum = combined_all(
        (local_max, local_total, taught), "expert", combine_stats
    )
    log_total = highest + jnp.log(totals)
    entropy = jnp.sum(teacher_probs * jnp.log(teacher_probs), axis=1)
    terms = 2.0 * log_total - picked_sum + entropy
    loss_part = (
        jnp.sum(lax.dynamic_slice_in_dim(terms, my_index * loss_local, loss_local, 0)) / loss_count
    )
    loss_rows = logits.shape[0]
    target_rows = math.gcd(loss_rows, 128)

    def target_block(triple):
        target_block_ids, teacher_block_ids, prob_block = triple
        hit_target = (target_block_ids[:, None] == vocab_iota[None, :]).astype(jnp.float32)
        hit_teacher = jnp.sum(
            jnp.where(
                teacher_block_ids[:, :, None] == vocab_iota[None, None, :],
                prob_block[:, :, None],
                0.0,
            ),
            axis=1,
        )
        return hit_target + hit_teacher

    taken = lax.map(
        target_block,
        (
            target_local.reshape(-1, target_rows),
            teacher_local.reshape(-1, target_rows, teacher_ids.shape[1]),
            teacher_probs.reshape(-1, target_rows, teacher_ids.shape[1]),
        ),
    ).reshape(loss_rows, vocab_rows)
    soft = jnp.exp(logits - log_total[:, None])
    logit_grad = ((2.0 * soft - taken) / loss_count).astype(jnp.bfloat16)
    embed_head = jnp.einsum(
        "gv,gd->vd", logit_grad, group_final, preferred_element_type=jnp.float32
    )
    final_grad = lax.psum_scatter(
        jnp.dot(logit_grad, table_low, preferred_element_type=jnp.float32),
        "expert",
        scatter_dimension=0,
        tiled=True,
    )
    final_full = jnp.zeros((local_rows, width), jnp.float32).at[positions].add(final_grad)
    grad_two, gain_three = norm_backward(normal_three, factor_three, gain_rows[2], final_full)
    gate_grad = jnp.sum(grad_two[:, None, :] * picked, axis=2)
    chosen_grad = gating * (gate_grad - jnp.sum(gating * gate_grad, axis=1, keepdims=True))
    expert_ids = jnp.arange(experts, dtype=jnp.int32)
    route_grad = jnp.sum(
        chosen_grad[:, :, None] * (own_routes[:, :, None] == expert_ids[None, None, :]), axis=1
    )
    router_grad = jnp.dot(route_grad.T, moe_float, precision=highest_precision)
    moe_grad = jnp.dot(route_grad, router, precision=highest_precision)
    result_grad = (
        (gating[:, :, None] * grad_two[:, None, :])
        .astype(jnp.bfloat16)
        .reshape(local_rows * TOP, width)
    )
    outgoing_grad = (
        jnp.zeros((experts * capacity, width), jnp.bfloat16).at[landing].set(result_grad)
    )
    arrived_grad = lax.all_to_all(
        outgoing_grad.reshape(members, local_experts, capacity, width),
        "expert",
        split_axis=0,
        concat_axis=2,
        tiled=True,
    )
    arrived_grad = arrived_grad.reshape(local_experts, members * capacity, width)
    out_grad = jnp.einsum(
        "ecf,ecd->efd", activated, arrived_grad, preferred_element_type=jnp.float32
    )
    activated_grad = jnp.einsum(
        "ecd,efd->ecf", arrived_grad, out_low, preferred_element_type=jnp.float32
    )
    gelu_pull = jax.vjp(lambda inner: jax.nn.gelu(inner, approximate=True), expert_hidden)[1]
    hidden_grad = gelu_pull(activated_grad)[0].astype(jnp.bfloat16)
    in_grad = jnp.einsum("ecd,ecf->edf", arrived, hidden_grad, preferred_element_type=jnp.float32)
    rows_grad = jnp.einsum("ecf,edf->ecd", hidden_grad, in_low, preferred_element_type=jnp.float32)
    back_rows = lax.all_to_all(
        rows_grad.reshape(local_experts, members, capacity, width),
        "expert",
        split_axis=1,
        concat_axis=0,
        tiled=True,
    )
    back_rows = back_rows.reshape(experts * capacity, width)
    moe_grad = moe_grad + jnp.sum(
        jnp.take(back_rows, landing, axis=0).reshape(local_rows, TOP, width), axis=1
    )
    grad_part, gain_two = norm_backward(normal_two, factor_two, gain_rows[1], moe_grad)
    grad_one = grad_two + grad_part
    attn_grad = grad_one.astype(jnp.bfloat16)
    out_weight_grad = jnp.einsum("tc,td->cd", mixed, attn_grad, preferred_element_type=jnp.float32)
    mixed_grad = jnp.einsum(
        "td,cd->tc", attn_grad, dense_low[3], preferred_element_type=jnp.float32
    )
    mixed_grad = mixed_grad.astype(jnp.bfloat16).reshape(local_rows, head_count, HEAD)

    def backward_block(carry, inputs):
        keys_grad, values_grad = carry
        block_index, log_block = inputs
        scores, query_block, key_block, first_row = block_scores(
            query, keys, seg_ids, block_index, length, block_rows, scaling
        )
        soft_block = jnp.exp(scores - log_block[..., None])
        value_part = jnp.einsum(
            "hqk,qhd->khd",
            soft_block.astype(jnp.bfloat16),
            mixed_grad,
            preferred_element_type=jnp.float32,
        )
        weight_grad = jnp.einsum(
            "qhd,khd->hqk", mixed_grad, values, preferred_element_type=jnp.float32
        )
        score_grad = soft_block * (
            weight_grad - jnp.sum(soft_block * weight_grad, axis=-1, keepdims=True)
        )
        score_grad = score_grad.astype(jnp.bfloat16)
        query_part = (
            jnp.einsum("hqk,khd->qhd", score_grad, key_block, preferred_element_type=jnp.float32)
            * scaling
        )
        key_part = (
            jnp.einsum("hqk,qhd->khd", score_grad, query_block, preferred_element_type=jnp.float32)
            * scaling
        )
        keys_grad = keys_grad + key_part
        values_grad = values_grad + value_part
        return ((keys_grad, values_grad), query_part)

    zero_grad = jnp.zeros((local_rows, head_count, HEAD), jnp.float32)
    (keys_grad, values_grad), query_parts = lax.scan(
        backward_block, (zero_grad, zero_grad), (jnp.arange(block_count), log_totals)
    )
    projected_grad = jnp.stack(
        [
            query_parts.reshape(local_rows, width),
            keys_grad.reshape(local_rows, width),
            values_grad.reshape(local_rows, width),
        ]
    ).astype(jnp.bfloat16)
    qkv_grad = jnp.einsum(
        "td,jte->jde", attn_in, projected_grad, preferred_element_type=jnp.float32
    )
    attn_in_grad = jnp.einsum(
        "jte,jde->td", projected_grad, dense_low[:3], preferred_element_type=jnp.float32
    )
    grad_part, gain_one = norm_backward(normal_one, factor_one, gain_rows[0], attn_in_grad)
    stream_grad = (grad_one + grad_part).astype(jnp.bfloat16)
    group_grad = lax.all_gather(stream_grad, "expert", axis=0, tiled=True)

    def add_rows(total, pair):
        selector = (pair[0][:, None] == vocab_iota[None, :]).astype(jnp.bfloat16)
        return (
            total + jnp.einsum("tv,td->vd", selector, pair[1], preferred_element_type=jnp.float32),
            None,
        )

    embed_grad, _ = lax.scan(
        add_rows,
        embed_head,
        (id_blocks, group_grad.reshape(group_count // lookup_rows, lookup_rows, width)),
    )
    in_sum, out_sum, embed_sum = (
        lax.psum_scatter(
            in_grad.astype(jnp.bfloat16), "dp", scatter_dimension=1, tiled=True
        ).astype(jnp.float32),
        lax.psum_scatter(
            out_grad.astype(jnp.bfloat16), "dp", scatter_dimension=1, tiled=True
        ).astype(jnp.float32),
        lax.psum_scatter(
            embed_grad.astype(jnp.bfloat16), "dp", scatter_dimension=1, tiled=True
        ).astype(jnp.float32),
    )
    attention_grad = jnp.concatenate([qkv_grad, out_weight_grad[None]], axis=0)
    small_grad = jnp.concatenate([jnp.stack([gain_one, gain_two, gain_three]), router_grad], axis=0)
    attention_sum, small_sum, loss_value = lax.psum(
        (attention_grad, small_grad, loss_part), ("dp", "expert")
    )
    share = width // replicas
    share_start = lax.axis_index("dp") * share
    attention_sum = lax.dynamic_slice_in_dim(attention_sum, share_start, share, 1)
    small_sum = lax.dynamic_slice_in_dim(small_sum, share_start, share, 1)
    rate_base = loss_count**0.5
    first_out = nesterov_update(
        attention, attention_moment, attention_average, attention_sum, RATE_TABLE[0] * rate_base
    )
    second_out = nesterov_update(
        expert_in, expert_in_moment, expert_in_average, in_sum, RATE_TABLE[1] * rate_base
    )
    third_out = nesterov_update(
        expert_out, expert_out_moment, expert_out_average, out_sum, RATE_TABLE[2] * rate_base
    )
    fourth_out = nesterov_update(
        embedding, embedding_moment, embedding_average, embed_sum, RATE_TABLE[3] * rate_base
    )
    fifth_out = nesterov_update(
        small_params, small_moment, small_average, small_sum, RATE_TABLE[4] * rate_base
    )
    return (loss_value,) + first_out + second_out + third_out + fourth_out + fifth_out


def solution(mesh):
    return jax.shard_map(
        shards,
        mesh=mesh,
        in_specs=(
            P("dp", None),
            P(("dp", "expert"), None),
            P("dp", None, None),
            P(("dp", "expert")),
            P("dp"),
            P("dp", None),
            P("dp", None),
            P(None, "dp", None),
            P(None, "dp", None),
            P(None, "dp", None),
            P("expert", "dp", None),
            P("expert", "dp", None),
            P("expert", "dp", None),
            P("expert", "dp", None),
            P("expert", "dp", None),
            P("expert", "dp", None),
            P("expert", "dp"),
            P("expert", "dp"),
            P("expert", "dp"),
            P(None, "dp"),
            P(None, "dp"),
            P(None, "dp"),
        ),
        out_specs=(
            P(),
            P(None, "dp", None),
            P(None, "dp", None),
            P(None, "dp", None),
            P(None, "dp", None),
            P("expert", "dp", None),
            P("expert", "dp", None),
            P("expert", "dp", None),
            P("expert", "dp", None),
            P("expert", "dp", None),
            P("expert", "dp", None),
            P("expert", "dp", None),
            P("expert", "dp", None),
            P("expert", "dp"),
            P("expert", "dp"),
            P("expert", "dp"),
            P("expert", "dp"),
            P(None, "dp"),
            P(None, "dp"),
            P(None, "dp"),
            P(None, "dp"),
        ),
        check_vma=False,
    )
```

```python
import math

import jax
import jax.numpy as jnp
from jax import lax
from jax.sharding import PartitionSpec as P

HEAD = 64
TOP = 2
STEP = 7


EPSILON = 1e-06
MOMENTUM = 0.9
RATE_TABLE = (0.1, 0.3, 0.01, 0.05, 0.05)
MASKED_SCORE = -1e30


def partner_order(members):
    if members & (members - 1) == 0:
        return [[(i, i ^ k) for i in range(members)] for k in range(members)]
    return [[(i, (k - i) % members) for i in range(members)] for k in range(members)]


def partner_of(me, k, members):
    return me ^ k if members & (members - 1) == 0 else (k - me) % members


def swap(value, k, members):
    return value if k == 0 else lax.ppermute(value, "expert", partner_order(members)[k])


def in_order(parts, me):
    members = len(parts)
    stacked = jnp.stack(parts)
    return jnp.stack(
        [
            lax.dynamic_index_in_dim(stacked, partner_of(me, k, members), 0, keepdims=False)
            for k in range(members)
        ]
    )


def shared(value, members):
    return [swap(value, k, members) for k in range(members)]


def normal_parts(stream):
    factor = lax.rsqrt(jnp.mean(stream * stream, axis=-1, keepdims=True) + EPSILON)
    return (stream * factor, factor)


def norm_backward(normal, factor, gain, grad):
    gain_grad = jnp.sum(grad * normal, axis=0)
    normal_grad = grad * gain
    inner = jnp.mean(normal_grad * normal, axis=-1, keepdims=True)
    return (factor * (normal_grad - normal * inner), gain_grad)


def slot_table(block_routes, experts):
    flat = block_routes.reshape(-1)
    hits = (flat[:, None] == jnp.arange(experts, dtype=jnp.int32)[None, :]).astype(jnp.int32)
    place = jnp.arange(flat.shape[0], dtype=jnp.int32)
    earlier = (place[None, :] < place[:, None]).astype(jnp.bfloat16)
    before = jnp.dot(earlier, hits.astype(jnp.bfloat16), preferred_element_type=jnp.float32)
    return jnp.sum(before.astype(jnp.int32) * hits, axis=1).reshape(block_routes.shape)


def block_scores(query, keys, seg_ids, block_index, length, block_rows, scaling):
    start = block_index * block_rows
    first_row = start // length * length
    scores = jnp.einsum("qhd,khd->hqk", query, keys, preferred_element_type=jnp.float32) * scaling
    query_place = start - first_row + jnp.arange(block_rows)
    allowed = (jnp.arange(length)[None, :] <= query_place[:, None]) & (
        seg_ids[None, :] == seg_ids[:, None]
    )
    return (jnp.where(allowed[None], scores, MASKED_SCORE), query, keys, first_row)


def label_weights(ids, weights, vocab_rows):
    lanes = 128
    tiles = (vocab_rows + lanes - 1) // lanes
    parts = []
    rest = weights
    for _ in range(3):
        part = lax.reduce_precision(rest, 8, 7)
        parts.append(part)
        rest = rest - part
    high = jnp.arange(tiles, dtype=jnp.int32)
    low = jnp.arange(lanes, dtype=jnp.int32)
    high_hits = (ids >> 7)[:, :, None] == high[None, None, :]
    rows = jnp.concatenate(
        [jnp.where(high_hits, part[:, :, None], 0.0).astype(jnp.bfloat16) for part in parts], axis=1
    )
    columns = ((ids & (lanes - 1))[:, :, None] == low[None, None, :]).astype(jnp.bfloat16)
    columns = jnp.concatenate([columns] * len(parts), axis=1)
    spread = jnp.einsum("pih,pil->phl", rows, columns, preferred_element_type=jnp.float32)
    return spread.reshape(ids.shape[0], tiles * lanes)[:, :vocab_rows]


def nesterov_update(master, moment, average, grad, rate):
    moment_next = MOMENTUM * moment + grad
    master_next = master - rate * (grad + MOMENTUM * moment_next)
    average_next = average + (master_next - average) / (STEP + 1)
    return (master_next, moment_next, average_next, master_next.astype(jnp.bfloat16))


def shards(
    token_ids,
    segments,
    routes,
    positions,
    targets,
    teacher_ids,
    teacher_probs,
    attention,
    attention_moment,
    attention_average,
    expert_in,
    expert_in_moment,
    expert_in_average,
    expert_out,
    expert_out_moment,
    expert_out_average,
    embedding,
    embedding_moment,
    embedding_average,
    small_params,
    small_moment,
    small_average,
):
    members = lax.axis_size("expert")
    replicas = lax.axis_size("dp")
    my_index = lax.axis_index("expert")
    length = segments.shape[1]
    local_rows = segments.shape[0] * length
    width = attention.shape[2]
    head_count = width // HEAD
    local_experts = expert_in.shape[0]
    experts = local_experts * members
    vocab_rows = embedding.shape[0]
    capacity = max(2, 3 * local_rows * TOP // (2 * experts))
    loss_local = positions.shape[0]
    loss_count = loss_local * members * replicas
    block_rows = min(512, length)
    block_count = local_rows // block_rows
    scaling = HEAD ** (-0.5)
    highest_precision = lax.Precision.HIGHEST
    group_count = members * local_rows
    lookup_rows = math.gcd(group_count, 2048)
    vocab_iota = jnp.arange(vocab_rows, dtype=jnp.int32)
    share = width // replicas
    chunk = attention.shape[0] * share // members
    small_rows = small_params.size // width + 1
    small_flat = jnp.pad(
        small_params.reshape(-1), (0, small_rows * width - small_params.size)
    ).reshape(small_rows, width)
    dense_part = lax.dynamic_slice_in_dim(
        attention.reshape(attention.shape[0] * share, width), my_index * chunk, chunk, 0
    )
    dense_part = lax.all_gather(
        jnp.concatenate([dense_part, small_flat], axis=0).astype(jnp.bfloat16), "dp", axis=0
    )
    small_low = dense_part[:, chunk:].reshape(replicas, small_rows * width)
    small_low = small_low[:, : small_params.size].reshape(replicas, small_params.shape[0], share)
    small_low = small_low.transpose(1, 0, 2).reshape(small_params.shape[0], width)
    dense_parts = in_order(shared(dense_part[:, :chunk], members), my_index)
    dense_low = (
        dense_parts.transpose(1, 0, 2, 3)
        .reshape(replicas, attention.shape[0], share, width)
        .transpose(1, 0, 2, 3)
        .reshape(attention.shape[0], width, width)
    )
    in_low, out_low, table_low = (
        lax.all_gather(expert_in.astype(jnp.bfloat16), "dp", axis=1, tiled=True),
        lax.all_gather(expert_out.astype(jnp.bfloat16), "dp", axis=1, tiled=True),
        lax.all_gather(embedding.astype(jnp.bfloat16), "dp", axis=1, tiled=True),
    )
    gain_rows = small_low[:3].astype(jnp.float32)
    router = small_low[3:].astype(jnp.float32)
    group_ids = token_ids.reshape(-1)
    own_routes = lax.dynamic_slice_in_dim(
        routes.reshape(members * local_rows, TOP), my_index * local_rows, local_rows, 0
    )
    local_ids = group_ids - my_index * vocab_rows
    id_blocks = local_ids.reshape(group_count // lookup_rows, lookup_rows)
    own_ids = lax.dynamic_slice_in_dim(group_ids, my_index * local_rows, local_rows, 0)
    column_ids = lax.all_gather(own_ids, "dp", axis=0, tiled=True)
    rows_table = jnp.concatenate(shared(embedding.astype(jnp.bfloat16), members), axis=0)
    places = partner_of(my_index, column_ids // vocab_rows, members) * vocab_rows
    places = places + column_ids % vocab_rows
    stream_parts = jnp.take(rows_table, places, axis=0, mode="clip")
    stream = lax.all_to_all(
        stream_parts, "dp", split_axis=0, concat_axis=1, tiled=True
    ).astype(jnp.float32)
    normal_one, factor_one = normal_parts(stream)
    attn_in = (normal_one * gain_rows[0]).astype(jnp.bfloat16)
    projected = jnp.einsum(
        "td,jde->jte", attn_in, dense_low[:3], preferred_element_type=jnp.float32
    ).astype(jnp.bfloat16)
    query = projected[0].reshape(local_rows, head_count, HEAD)
    keys = projected[1].reshape(local_rows, head_count, HEAD)
    values = projected[2].reshape(local_rows, head_count, HEAD)
    seg_ids = segments.reshape(-1)

    def forward_block(block_index):
        scores, query_block, key_block, first_row = block_scores(
            query, keys, seg_ids, block_index, length, block_rows, scaling
        )
        highest = jnp.max(scores, axis=-1, keepdims=True)
        powers = jnp.exp(scores - highest)
        totals = jnp.sum(powers, axis=-1, keepdims=True)
        mixed_block = jnp.einsum(
            "hqk,khd->qhd",
            (powers / totals).astype(jnp.bfloat16),
            values,
            preferred_element_type=jnp.float32,
        )
        return (mixed_block, (highest + jnp.log(totals))[..., 0])

    mixed_blocks, log_totals = lax.map(forward_block, jnp.arange(block_count))
    mixed = mixed_blocks.reshape(local_rows, width).astype(jnp.bfloat16)
    hidden_one = stream + jnp.dot(mixed, dense_low[3], preferred_element_type=jnp.float32)
    normal_two, factor_two = normal_parts(hidden_one)
    moe_in = (normal_two * gain_rows[1]).astype(jnp.bfloat16)
    moe_float = moe_in.astype(jnp.float32)
    router_logits = jnp.dot(moe_float, router.T, precision=highest_precision)
    expert_ids = jnp.arange(experts, dtype=jnp.int32)
    route_hits = (own_routes[:, :, None] == expert_ids[None, None, :]).astype(jnp.float32)
    chosen = jnp.sum(router_logits[:, None, :] * route_hits, axis=2)
    gating = jnp.exp(chosen - jnp.max(chosen, axis=1, keepdims=True))
    gating = gating / jnp.sum(gating, axis=1, keepdims=True)
    slots = slot_table(own_routes, experts)
    block = local_experts * capacity
    landing = partner_of(my_index, own_routes // local_experts, members) * block
    landing = landing + own_routes % local_experts * capacity + slots
    landing_iota = jnp.arange(members * block, dtype=jnp.int32)
    picks = [
        (landing[:, j][:, None] == landing_iota[None, :]).astype(jnp.bfloat16) for j in range(TOP)
    ]
    any_pick = sum(picks)

    def exchanged(rows):
        parts = rows.reshape(members, block, rows.shape[1])
        return jnp.stack([swap(parts[k], k, members) for k in range(members)])

    outgoing = jnp.einsum("tr,td->rd", any_pick, moe_in, preferred_element_type=jnp.float32)
    arrived = exchanged(outgoing.astype(jnp.bfloat16))
    arrived = (
        arrived.reshape(members, local_experts, capacity, width)
        .transpose(1, 0, 2, 3)
        .reshape(local_experts, members * capacity, width)
    )

    def sent_back(rows):
        rows = rows.reshape(local_experts, members, capacity, width).transpose(1, 0, 2, 3)
        return exchanged(rows.reshape(members * block, width)).reshape(members * block, width)

    expert_hidden = jnp.einsum("ecd,edf->ecf", arrived, in_low, preferred_element_type=jnp.float32)
    activated = jax.nn.gelu(expert_hidden, approximate=True).astype(jnp.bfloat16)
    expert_result = jnp.einsum(
        "ecf,efd->ecd", activated, out_low, preferred_element_type=jnp.float32
    ).astype(jnp.bfloat16)
    returned = sent_back(expert_result)
    picked = [jnp.dot(pick, returned, preferred_element_type=jnp.float32) for pick in picks]
    hidden_two = hidden_one + sum(gating[:, j][:, None] * picked[j] for j in range(TOP))
    normal_three, factor_three = normal_parts(hidden_two)
    final = (normal_three * gain_rows[2]).astype(jnp.bfloat16)
    place_hits = positions[:, None] == jnp.arange(local_rows, dtype=jnp.int32)[None, :]
    final_rows = jnp.dot(
        place_hits.astype(jnp.bfloat16), final, preferred_element_type=jnp.float32
    ).astype(jnp.bfloat16)
    group_final = lax.all_gather(final_rows, "expert", axis=0, tiled=True)
    logits = jnp.einsum("gd,vd->gv", group_final, table_low, preferred_element_type=jnp.float32)
    target_local = targets - my_index * vocab_rows
    teacher_local = teacher_ids - my_index * vocab_rows
    taken = label_weights(
        jnp.concatenate([teacher_local, target_local[:, None]], axis=1),
        jnp.concatenate([teacher_probs, jnp.ones_like(teacher_probs[:, :1])], axis=1),
        vocab_rows,
    )
    taught = jnp.sum(taken * logits, axis=1)
    local_max = jnp.max(logits, axis=1)
    local_total = jnp.sum(jnp.exp(logits - local_max[:, None]), axis=1)
    stats = lax.all_gather(jnp.stack([local_max, local_total, taught]), "expert")
    highest = jnp.max(stats[:, 0], axis=0)
    totals = jnp.sum(stats[:, 1] * jnp.exp(stats[:, 0] - highest[None]), axis=0)
    picked_sum = jnp.sum(stats[:, 2], axis=0)
    log_total = highest + jnp.log(totals)
    entropy = jnp.sum(teacher_probs * jnp.log(teacher_probs), axis=1)
    terms = 2.0 * log_total - picked_sum + entropy
    loss_part = (
        jnp.sum(lax.dynamic_slice_in_dim(terms, my_index * loss_local, loss_local, 0)) / loss_count
    )
    soft = jnp.exp(logits - log_total[:, None])
    logit_grad = ((2.0 * soft - taken) / loss_count).astype(jnp.bfloat16)
    embed_head = jnp.einsum(
        "gv,gd->vd", logit_grad, group_final, preferred_element_type=jnp.float32
    )
    final_parts = jnp.dot(logit_grad, table_low, preferred_element_type=jnp.float32)
    final_grad = sum(
        swap(
            lax.dynamic_slice_in_dim(
                final_parts, partner_of(my_index, k, members) * loss_local, loss_local, 0
            ),
            k,
            members,
        )
        for k in range(members)
    )
    final_full = jnp.dot(
        place_hits.astype(jnp.float32).T, final_grad, precision=highest_precision
    )
    grad_two, gain_three = norm_backward(normal_three, factor_three, gain_rows[2], final_full)
    gate_grad = jnp.stack([jnp.sum(grad_two * part, axis=1) for part in picked], axis=1)
    chosen_grad = gating * (gate_grad - jnp.sum(gating * gate_grad, axis=1, keepdims=True))
    route_grad = jnp.sum(chosen_grad[:, :, None] * route_hits, axis=1)
    router_grad = jnp.dot(route_grad.T, moe_float, precision=highest_precision)
    moe_grad = jnp.dot(route_grad, router, precision=highest_precision)
    outgoing_grad = sum(
        jnp.einsum(
            "tr,td->rd",
            picks[j],
            (gating[:, j][:, None] * grad_two).astype(jnp.bfloat16),
            preferred_element_type=jnp.float32,
        )
        for j in range(TOP)
    ).astype(jnp.bfloat16)
    arrived_grad = (
        exchanged(outgoing_grad)
        .reshape(members, local_experts, capacity, width)
        .transpose(1, 0, 2, 3)
        .reshape(local_experts, members * capacity, width)
    )
    out_grad = jnp.einsum(
        "ecf,ecd->efd", activated, arrived_grad, preferred_element_type=jnp.float32
    )
    activated_grad = jnp.einsum(
        "ecd,efd->ecf", arrived_grad, out_low, preferred_element_type=jnp.float32
    )
    gelu_pull = jax.vjp(lambda inner: jax.nn.gelu(inner, approximate=True), expert_hidden)[1]
    hidden_grad = gelu_pull(activated_grad)[0].astype(jnp.bfloat16)
    in_grad = jnp.einsum("ecd,ecf->edf", arrived, hidden_grad, preferred_element_type=jnp.float32)
    rows_grad = jnp.einsum("ecf,edf->ecd", hidden_grad, in_low, preferred_element_type=jnp.float32)
    back_rows = sent_back(rows_grad.astype(jnp.bfloat16))
    moe_grad = moe_grad + jnp.dot(any_pick, back_rows, preferred_element_type=jnp.float32)
    grad_part, gain_two = norm_backward(normal_two, factor_two, gain_rows[1], moe_grad)
    grad_one = grad_two + grad_part
    attn_grad = grad_one.astype(jnp.bfloat16)
    out_weight_grad = jnp.einsum("tc,td->cd", mixed, attn_grad, preferred_element_type=jnp.float32)
    mixed_grad = jnp.einsum(
        "td,cd->tc", attn_grad, dense_low[3], preferred_element_type=jnp.float32
    )
    mixed_grad = mixed_grad.astype(jnp.bfloat16).reshape(local_rows, head_count, HEAD)

    def backward_block(carry, inputs):
        keys_grad, values_grad = carry
        block_index, log_block = inputs
        scores, query_block, key_block, first_row = block_scores(
            query, keys, seg_ids, block_index, length, block_rows, scaling
        )
        soft_block = jnp.exp(scores - log_block[..., None])
        value_part = jnp.einsum(
            "hqk,qhd->khd",
            soft_block.astype(jnp.bfloat16),
            mixed_grad,
            preferred_element_type=jnp.float32,
        )
        weight_grad = jnp.einsum(
            "qhd,khd->hqk", mixed_grad, values, preferred_element_type=jnp.float32
        )
        score_grad = soft_block * (
            weight_grad - jnp.sum(soft_block * weight_grad, axis=-1, keepdims=True)
        )
        score_grad = score_grad.astype(jnp.bfloat16)
        query_part = (
            jnp.einsum("hqk,khd->qhd", score_grad, key_block, preferred_element_type=jnp.float32)
            * scaling
        )
        key_part = (
            jnp.einsum("hqk,qhd->khd", score_grad, query_block, preferred_element_type=jnp.float32)
            * scaling
        )
        keys_grad = keys_grad + key_part
        values_grad = values_grad + value_part
        return ((keys_grad, values_grad), query_part)

    zero_grad = jnp.zeros((local_rows, head_count, HEAD), jnp.float32)
    (keys_grad, values_grad), query_parts = lax.scan(
        backward_block, (zero_grad, zero_grad), (jnp.arange(block_count), log_totals)
    )
    projected_grad = jnp.stack(
        [
            query_parts.reshape(local_rows, width),
            keys_grad.reshape(local_rows, width),
            values_grad.reshape(local_rows, width),
        ]
    ).astype(jnp.bfloat16)
    qkv_grad = jnp.einsum(
        "td,jte->jde", attn_in, projected_grad, preferred_element_type=jnp.float32
    )
    attn_in_grad = jnp.einsum(
        "jte,jde->td", projected_grad, dense_low[:3], preferred_element_type=jnp.float32
    )
    grad_part, gain_one = norm_backward(normal_one, factor_one, gain_rows[0], attn_in_grad)
    stream_grad = (grad_one + grad_part).astype(jnp.bfloat16)
    group_grad = jnp.concatenate(shared(stream_grad, members), axis=0)
    id_blocks = jnp.stack(in_order(list(local_ids.reshape(members, local_rows)), my_index))
    id_blocks = id_blocks.reshape(group_count // lookup_rows, lookup_rows)

    def add_rows(total, pair):
        selector = (pair[0][:, None] == vocab_iota[None, :]).astype(jnp.bfloat16)
        return (
            total + jnp.einsum("tv,td->vd", selector, pair[1], preferred_element_type=jnp.float32),
            None,
        )

    embed_grad, _ = lax.scan(
        add_rows,
        embed_head,
        (id_blocks, group_grad.reshape(group_count // lookup_rows, lookup_rows, width)),
    )
    in_sum, out_sum, embed_sum = (
        lax.psum_scatter(
            in_grad.astype(jnp.bfloat16), "dp", scatter_dimension=1, tiled=True
        ).astype(jnp.float32),
        lax.psum_scatter(
            out_grad.astype(jnp.bfloat16), "dp", scatter_dimension=1, tiled=True
        ).astype(jnp.float32),
        lax.psum_scatter(
            embed_grad.astype(jnp.bfloat16), "dp", scatter_dimension=1, tiled=True
        ).astype(jnp.float32),
    )
    attention_grad = jnp.concatenate([qkv_grad, out_weight_grad[None]], axis=0)
    small_grad = jnp.concatenate([jnp.stack([gain_one, gain_two, gain_three]), router_grad], axis=0)
    dense_grads = (
        attention_grad.reshape(attention.shape[0], replicas, share, width)
        .transpose(1, 0, 2, 3)
        .reshape(replicas, members, chunk, width)
        .astype(jnp.bfloat16)
    )
    dense_sum = sum(
        swap(
            lax.dynamic_index_in_dim(
                dense_grads, partner_of(my_index, k, members), 1, keepdims=False
            ),
            k,
            members,
        ).astype(jnp.float32)
        for k in range(members)
    )
    small_grads = small_grad.reshape(-1, replicas, share).transpose(1, 0, 2).reshape(replicas, -1)
    small_grads = jnp.concatenate(
        [
            small_grads,
            jnp.full((replicas, 1), loss_part),
            jnp.zeros((replicas, small_rows * width - small_params.size - 1), jnp.float32),
        ],
        axis=1,
    ).reshape(replicas, small_rows, width)
    small_grads = sum(shared(small_grads, members))
    summed = lax.psum_scatter(
        jnp.concatenate([dense_sum, small_grads], axis=1), "dp", scatter_dimension=0
    )
    small_sum = summed[chunk:].reshape(-1)
    loss_value = small_sum[small_params.size]
    small_sum = small_sum[: small_params.size].reshape(small_params.shape[0], share)
    attention_sum = in_order(shared(summed[:chunk], members), my_index)
    attention_sum = attention_sum.reshape(attention.shape[0], share, width)
    rate_base = loss_count**0.5
    first_out = nesterov_update(
        attention, attention_moment, attention_average, attention_sum, RATE_TABLE[0] * rate_base
    )
    second_out = nesterov_update(
        expert_in, expert_in_moment, expert_in_average, in_sum, RATE_TABLE[1] * rate_base
    )
    third_out = nesterov_update(
        expert_out, expert_out_moment, expert_out_average, out_sum, RATE_TABLE[2] * rate_base
    )
    fourth_out = nesterov_update(
        embedding, embedding_moment, embedding_average, embed_sum, RATE_TABLE[3] * rate_base
    )
    fifth_out = nesterov_update(
        small_params, small_moment, small_average, small_sum, RATE_TABLE[4] * rate_base
    )
    return (loss_value,) + first_out + second_out + third_out + fourth_out + fifth_out


def solution(mesh):
    return jax.shard_map(
        shards,
        mesh=mesh,
        in_specs=(
            P("dp", None),
            P(("dp", "expert"), None),
            P("dp", None, None),
            P(("dp", "expert")),
            P("dp"),
            P("dp", None),
            P("dp", None),
            P(None, "dp", None),
            P(None, "dp", None),
            P(None, "dp", None),
            P("expert", "dp", None),
            P("expert", "dp", None),
            P("expert", "dp", None),
            P("expert", "dp", None),
            P("expert", "dp", None),
            P("expert", "dp", None),
            P("expert", "dp"),
            P("expert", "dp"),
            P("expert", "dp"),
            P(None, "dp"),
            P(None, "dp"),
            P(None, "dp"),
        ),
        out_specs=(
            P(),
            P(None, "dp", None),
            P(None, "dp", None),
            P(None, "dp", None),
            P(None, "dp", None),
            P("expert", "dp", None),
            P("expert", "dp", None),
            P("expert", "dp", None),
            P("expert", "dp", None),
            P("expert", "dp", None),
            P("expert", "dp", None),
            P("expert", "dp", None),
            P("expert", "dp", None),
            P("expert", "dp"),
            P("expert", "dp"),
            P("expert", "dp"),
            P("expert", "dp"),
            P(None, "dp"),
            P(None, "dp"),
            P(None, "dp"),
            P(None, "dp"),
        ),
        check_vma=False,
    )
```

```python
import math

import jax
import jax.numpy as jnp
from jax import lax
from jax.experimental import pallas as pl
from jax.experimental.pallas import tpu as pltpu
from jax.sharding import PartitionSpec as P

HEAD = 64
TOP = 2
STEP = 7


EPSILON = 1e-06
MOMENTUM = 0.9
RATE_TABLE = (0.1, 0.3, 0.01, 0.05, 0.05)
MASKED_SCORE = -1e30


def partner_order(members):
    if members & (members - 1) == 0:
        return [[(i, i ^ k) for i in range(members)] for k in range(members)]
    return [[(i, (k - i) % members) for i in range(members)] for k in range(members)]


def partner_of(me, k, members):
    return me ^ k if members & (members - 1) == 0 else (k - me) % members


def swap(value, k, members):
    return value if k == 0 else lax.ppermute(value, "expert", partner_order(members)[k])


def dp_swap(value, k, replicas):
    return lax.ppermute(value, "dp", [(i, i ^ k) for i in range(replicas)]) if k else value


def in_order(parts, me):
    members = len(parts)
    stacked = jnp.stack(parts)
    return jnp.stack(
        [
            lax.dynamic_index_in_dim(stacked, partner_of(me, k, members), 0, keepdims=False)
            for k in range(members)
        ]
    )


def shared(value, members):
    return [swap(value, k, members) for k in range(members)]


def normal_parts(stream):
    factor = lax.rsqrt(jnp.mean(stream * stream, axis=-1, keepdims=True) + EPSILON)
    return (stream * factor, factor)


def norm_backward(normal, factor, gain, grad):
    gain_grad = jnp.sum(grad * normal, axis=0)
    normal_grad = grad * gain
    inner = jnp.mean(normal_grad * normal, axis=-1, keepdims=True)
    return (factor * (normal_grad - normal * inner), gain_grad)


def slot_table(block_routes, experts):
    flat = block_routes.reshape(-1)
    hits = (flat[:, None] == jnp.arange(experts, dtype=jnp.int32)[None, :]).astype(jnp.int32)
    place = jnp.arange(flat.shape[0], dtype=jnp.int32)
    earlier = (place[None, :] < place[:, None]).astype(jnp.bfloat16)
    before = jnp.dot(earlier, hits.astype(jnp.bfloat16), preferred_element_type=jnp.float32)
    return jnp.sum(before.astype(jnp.int32) * hits, axis=1).reshape(block_routes.shape)


def block_scores(query, keys, seg_ids, block_index, length, block_rows, scaling):
    start = block_index * block_rows
    first_row = start // length * length
    scores = jnp.einsum("qhd,khd->hqk", query, keys, preferred_element_type=jnp.float32) * scaling
    query_place = start - first_row + jnp.arange(block_rows)
    allowed = (jnp.arange(length)[None, :] <= query_place[:, None]) & (
        seg_ids[None, :] == seg_ids[:, None]
    )
    return (jnp.where(allowed[None], scores, MASKED_SCORE), query, keys, first_row)


def in_thirds(values):
    parts = []
    for _ in range(3):
        part = lax.reduce_precision(values, 8, 7)
        parts.append(part)
        values = values - part
    return parts


def label_weights(ids, weights, vocab_rows):
    lanes = 128
    tiles = (vocab_rows + lanes - 1) // lanes
    parts = in_thirds(weights)
    high = jnp.arange(tiles, dtype=jnp.int32)
    low = jnp.arange(lanes, dtype=jnp.int32)
    high_hits = (ids >> 7)[:, :, None] == high[None, None, :]
    rows = jnp.concatenate(
        [jnp.where(high_hits, part[:, :, None], 0.0).astype(jnp.bfloat16) for part in parts], axis=1
    )
    columns = ((ids & (lanes - 1))[:, :, None] == low[None, None, :]).astype(jnp.bfloat16)
    columns = jnp.concatenate([columns] * len(parts), axis=1)
    spread = jnp.einsum("pih,pil->phl", rows, columns, preferred_element_type=jnp.float32)
    return spread.reshape(ids.shape[0], tiles * lanes)[:, :vocab_rows]


LANES = 128
WAYS = 4
GRID_ROWS = 32768
VMEM_LIMIT = 56 * 2**20


def add_rows_kernel(count_ref, row_ref, source_ref, *refs):
    pieces = len(refs) - 2 - WAYS
    grad_refs, out_ref, grads, sums = refs[:pieces], refs[pieces], refs[pieces + 1], refs[-WAYS:]
    start_ref = None
    if grad_refs[-1].dtype == jnp.float32:
        start_ref, grad_refs = grad_refs[-1], grad_refs[:-1]
    width, piece = grad_refs[0].shape
    pad = jnp.zeros((LANES - width, LANES), jnp.float32)
    for k, grad_ref in enumerate(grad_refs):

        def turn(i, _, k=k, grad_ref=grad_ref):
            lanes = pl.ds(pl.multiple_of(i * LANES, LANES), LANES)
            tile = jnp.concatenate([grad_ref[:, lanes].astype(jnp.float32), pad], axis=0)
            grads[pl.ds(pl.multiple_of(k * piece + i * LANES, LANES), LANES), :] = tile.T
            return 0

        lax.fori_loop(0, piece // LANES, turn, 0)
    step = 64
    for total in sums:

        def clear(i, _, total=total):
            total[pl.ds(pl.multiple_of(i * step, step), step), :] = jnp.zeros(
                (step, LANES), jnp.float32
            )
            return 0

        lax.fori_loop(0, total.shape[0] // step, clear, 0)

    def one_block(b, _):
        def one_step(i, _):
            for w in range(WAYS):
                row = row_ref[b, i * WAYS + w]
                source = source_ref[b, i * WAYS + w]
                sums[w][pl.ds(row, 1), :] += grads[pl.ds(source, 1), :]
            return 0

        return lax.fori_loop(0, count_ref[b], one_step, 0)

    lax.fori_loop(0, row_ref.shape[0], one_block, 0)

    def finish(i, _):
        place = pl.ds(pl.multiple_of(i * LANES, LANES), LANES)
        total = sum(part[place, :] for part in sums)
        if start_ref is None:
            out_ref[place, :] = total
        else:
            out_ref[:, place] = (total + start_ref[place, :]).T[:width]
        return 0

    lax.fori_loop(0, sums[0].shape[0] // LANES, finish, 0)


def row_lists(local_ids, vocab_rows, offset):
    ids = local_ids.reshape(-1, LANES)
    inside = (ids >= 0) & (ids < vocab_rows)
    place = jnp.arange(LANES, dtype=jnp.int32)
    earlier = (place[:, None] < place[None, :]).astype(jnp.bfloat16)
    before = jnp.dot(inside.astype(jnp.bfloat16), earlier, preferred_element_type=jnp.float32)
    chosen = inside[:, :, None] & (before.astype(jnp.int32)[:, :, None] == place[None, None, :])
    filled = jnp.sum(chosen.astype(jnp.int32), axis=1)
    rows = jnp.sum(jnp.where(chosen, ids[:, :, None], 0), axis=1)
    rows = jnp.where(filled > 0, rows, vocab_rows)
    origin = jnp.sum(jnp.where(chosen, place[None, :, None], 0), axis=1)
    origin = origin + offset + jnp.arange(ids.shape[0], dtype=jnp.int32)[:, None] * LANES
    counts = (jnp.sum(inside.astype(jnp.int32), axis=1) + WAYS - 1) // WAYS
    return counts, rows, origin


def add_rows(local_ids, grads, vocab_rows, start):
    width, piece = grads[0].shape
    if piece * len(grads) * 2 > GRID_ROWS or width > LANES or piece % LANES:
        vocab_iota = jnp.arange(vocab_rows, dtype=jnp.int32)
        total = jnp.zeros((width, vocab_rows), jnp.float32) if start is None else start
        for ids, part in zip(local_ids, grads):
            hits = (ids[:, None] == vocab_iota[None, :]).astype(jnp.bfloat16)
            total = total + jnp.dot(part, hits, preferred_element_type=jnp.float32)
        return total
    lists = [row_lists(ids, vocab_rows, k * piece) for k, ids in enumerate(local_ids)]
    lists = [jnp.concatenate(parts, axis=0) for parts in zip(*lists)]
    smem = pl.BlockSpec(memory_space=pltpu.SMEM)
    vmem = pl.BlockSpec(memory_space=pltpu.VMEM)
    padded_rows = -(-(vocab_rows + 1) // LANES) * LANES
    extra = [] if start is None else [start]
    shape = (padded_rows, LANES) if start is None else (width, padded_rows)
    summed = pl.pallas_call(
        add_rows_kernel,
        out_shape=jax.ShapeDtypeStruct(shape, jnp.float32),
        in_specs=[smem] * 3 + [vmem] * (len(grads) + len(extra)),
        out_specs=vmem,
        scratch_shapes=[pltpu.VMEM((len(grads) * piece, LANES), jnp.float32)]
        + [pltpu.VMEM((padded_rows, LANES), jnp.float32) for _ in range(WAYS)],
        compiler_params=pltpu.CompilerParams(vmem_limit_bytes=VMEM_LIMIT),
        cost_estimate=pl.CostEstimate(
            flops=len(grads) * piece * LANES * 8,
            bytes_accessed=4 * LANES * (2 * len(grads) * piece + 3 * WAYS * padded_rows) * 4,
            transcendentals=0,
        ),
    )(*lists, *grads, *extra)
    return summed if start is None else summed[:, :vocab_rows]


def nesterov_update(master, moment, average, grad, rate):
    moment_next = MOMENTUM * moment + grad
    master_next = master - rate * (grad + MOMENTUM * moment_next)
    average_next = average + (master_next - average) / (STEP + 1)
    return (master_next, moment_next, average_next, master_next.astype(jnp.bfloat16))


def shards(
    token_ids,
    segments,
    routes,
    positions,
    targets,
    teacher_ids,
    teacher_probs,
    attention,
    attention_moment,
    attention_average,
    expert_in,
    expert_in_moment,
    expert_in_average,
    expert_out,
    expert_out_moment,
    expert_out_average,
    embedding,
    embedding_moment,
    embedding_average,
    small_params,
    small_moment,
    small_average,
):
    members = lax.axis_size("expert")
    replicas = lax.axis_size("dp")
    my_index = lax.axis_index("expert")
    length = segments.shape[1]
    local_rows = segments.shape[0] * length
    width = attention.shape[2]
    head_count = width // HEAD
    local_experts = expert_in.shape[0]
    experts = local_experts * members
    vocab_rows = embedding.shape[0]
    capacity = max(2, 3 * local_rows * TOP // (2 * experts))
    loss_local = positions.shape[0]
    loss_count = loss_local * members * replicas
    block_rows = min(512, length)
    block_count = local_rows // block_rows
    scaling = HEAD ** (-0.5)
    highest_precision = lax.Precision.HIGHEST
    share = width // replicas
    chunk = attention.shape[0] * share // members
    small_rows = small_params.size // width + 1
    small_flat = jnp.pad(
        small_params.reshape(-1), (0, small_rows * width - small_params.size)
    ).reshape(small_rows, width)
    dense_part = lax.dynamic_slice_in_dim(
        attention.reshape(attention.shape[0] * share, width), my_index * chunk, chunk, 0
    )
    in_low, out_low, table_low = (
        lax.all_gather(expert_in.astype(jnp.bfloat16), "dp", axis=1, tiled=True),
        lax.all_gather(expert_out.astype(jnp.bfloat16), "dp", axis=1, tiled=True),
        lax.all_gather(embedding.astype(jnp.bfloat16), "dp", axis=1, tiled=True),
    )
    core = lax.axis_index("dp") & 1
    level = lax.axis_index("dp") >> 1
    levels = replicas // 2

    def by_core(value, axis):
        other = dp_swap(value, 1, replicas)
        first = jnp.where(core == 0, value, other)
        return jnp.stack([first, jnp.where(core == 0, other, value)], axis=axis)

    group_ids = token_ids.reshape(-1)
    own_routes = lax.dynamic_slice_in_dim(
        routes.reshape(members * local_rows, TOP), my_index * local_rows, local_rows, 0
    )
    target_local = targets - my_index * vocab_rows
    teacher_local = teacher_ids - my_index * vocab_rows
    taken = label_weights(
        jnp.concatenate([teacher_local, target_local[:, None]], axis=1),
        jnp.concatenate([teacher_probs, jnp.ones_like(teacher_probs[:, :1])], axis=1),
        vocab_rows,
    )
    rows_parts = shared(embedding.astype(jnp.bfloat16), members)
    dense_part = jnp.concatenate([dense_part, small_flat], axis=0).astype(jnp.bfloat16)
    dense_part, group_ids, rows_parts[1] = lax.optimization_barrier(
        (dense_part, group_ids, rows_parts[1])
    )
    level_ids = in_order([dp_swap(group_ids, 2 * k, replicas) for k in range(levels)], level)
    all_ids = by_core(level_ids, 1).reshape(replicas, members, local_rows)
    column_ids = lax.dynamic_index_in_dim(all_ids, my_index, 1, keepdims=False).reshape(-1)
    dense_part = in_order([dp_swap(dense_part, 2 * k, replicas) for k in range(levels)], level)
    rows_parts[-1], taken, dense_part = lax.optimization_barrier(
        (rows_parts[-1], taken, dense_part)
    )

    small_low = by_core(dense_part[:, chunk:], 1).reshape(replicas, small_rows * width)
    small_low = small_low[:, : small_params.size].reshape(replicas, small_params.shape[0], share)
    small_low = small_low.transpose(1, 0, 2).reshape(small_params.shape[0], width)
    gain_rows = small_low[:3].astype(jnp.float32)
    router = small_low[3:].astype(jnp.float32)
    rows_table = jnp.concatenate(rows_parts, axis=0)
    places = partner_of(my_index, column_ids // vocab_rows, members) * vocab_rows
    places = places + column_ids % vocab_rows
    stream_parts = jnp.take(rows_table, places, axis=0, mode="clip")
    dense_parts = shared(dense_part[:, :chunk], members)
    stream_parts, dense_parts = lax.optimization_barrier((stream_parts, dense_parts))
    dense_low = by_core(in_order(dense_parts, my_index), 2)
    dense_low = (
        dense_low.reshape(members, replicas, chunk, width)
        .transpose(1, 0, 2, 3)
        .reshape(replicas, attention.shape[0], share, width)
        .transpose(1, 0, 2, 3)
        .reshape(attention.shape[0], width, width)
    )
    stream = lax.all_to_all(
        stream_parts, "dp", split_axis=0, concat_axis=1, tiled=True
    ).astype(jnp.float32)
    normal_one, factor_one = normal_parts(stream)
    attn_in = (normal_one * gain_rows[0]).astype(jnp.bfloat16)
    projected = jnp.einsum(
        "td,jde->jte", attn_in, dense_low[:3], preferred_element_type=jnp.float32
    ).astype(jnp.bfloat16)
    query = projected[0].reshape(local_rows, head_count, HEAD)
    keys = projected[1].reshape(local_rows, head_count, HEAD)
    values = projected[2].reshape(local_rows, head_count, HEAD)
    seg_ids = segments.reshape(-1)

    def forward_block(block_index):
        scores, query_block, key_block, first_row = block_scores(
            query, keys, seg_ids, block_index, length, block_rows, scaling
        )
        highest = jnp.max(scores, axis=-1, keepdims=True)
        powers = jnp.exp(scores - highest)
        totals = jnp.sum(powers, axis=-1, keepdims=True)
        mixed_block = jnp.einsum(
            "hqk,khd->qhd",
            (powers / totals).astype(jnp.bfloat16),
            values,
            preferred_element_type=jnp.float32,
        )
        return (mixed_block, (highest + jnp.log(totals))[..., 0])

    mixed_blocks, log_totals = lax.map(forward_block, jnp.arange(block_count))
    mixed = mixed_blocks.reshape(local_rows, width).astype(jnp.bfloat16)
    hidden_one = stream + jnp.dot(mixed, dense_low[3], preferred_element_type=jnp.float32)
    normal_two, factor_two = normal_parts(hidden_one)
    moe_in = (normal_two * gain_rows[1]).astype(jnp.bfloat16)
    moe_float = moe_in.astype(jnp.float32)
    router_logits = jnp.dot(moe_float, router.T, precision=highest_precision)
    expert_ids = jnp.arange(experts, dtype=jnp.int32)
    route_hits = (own_routes[:, :, None] == expert_ids[None, None, :]).astype(jnp.float32)
    chosen = jnp.sum(router_logits[:, None, :] * route_hits, axis=2)
    gating = jnp.exp(chosen - jnp.max(chosen, axis=1, keepdims=True))
    gating = gating / jnp.sum(gating, axis=1, keepdims=True)
    slots = slot_table(own_routes, experts)
    block = local_experts * capacity
    landing = partner_of(my_index, own_routes // local_experts, members) * block
    landing = landing + own_routes % local_experts * capacity + slots
    landing_iota = jnp.arange(members * block, dtype=jnp.int32)
    picks = [
        (landing[:, j][:, None] == landing_iota[None, :]).astype(jnp.bfloat16) for j in range(TOP)
    ]
    any_pick = sum(picks)

    def exchanged(rows):
        parts = rows.reshape(members, block, rows.shape[1])
        return jnp.stack([swap(parts[k], k, members) for k in range(members)])

    outgoing = jnp.einsum("tr,td->rd", any_pick, moe_in, preferred_element_type=jnp.float32)
    arrived = exchanged(outgoing.astype(jnp.bfloat16))
    arrived = (
        arrived.reshape(members, local_experts, capacity, width)
        .transpose(1, 0, 2, 3)
        .reshape(local_experts, members * capacity, width)
    )

    def sent_back(rows):
        rows = rows.reshape(local_experts, members, capacity, width).transpose(1, 0, 2, 3)
        return exchanged(rows.reshape(members * block, width)).reshape(members * block, width)

    expert_hidden = jnp.einsum("ecd,edf->ecf", arrived, in_low, preferred_element_type=jnp.float32)
    activated = jax.nn.gelu(expert_hidden, approximate=True).astype(jnp.bfloat16)
    expert_result = jnp.einsum(
        "ecf,efd->ecd", activated, out_low, preferred_element_type=jnp.float32
    ).astype(jnp.bfloat16)
    returned = sent_back(expert_result)
    picked = [jnp.dot(pick, returned, preferred_element_type=jnp.float32) for pick in picks]
    hidden_two = hidden_one + sum(gating[:, j][:, None] * picked[j] for j in range(TOP))
    normal_three, factor_three = normal_parts(hidden_two)
    final = (normal_three * gain_rows[2]).astype(jnp.bfloat16)
    place_hits = positions[:, None] == jnp.arange(local_rows, dtype=jnp.int32)[None, :]
    final_rows = jnp.dot(
        place_hits.astype(jnp.bfloat16), final, preferred_element_type=jnp.float32
    ).astype(jnp.bfloat16)
    group_final = lax.all_gather(final_rows, "expert", axis=0, tiled=True)
    logits = jnp.einsum("gd,vd->gv", group_final, table_low, preferred_element_type=jnp.float32)
    taught = jnp.sum(taken * logits, axis=1)
    local_max = jnp.max(logits, axis=1)
    local_total = jnp.sum(jnp.exp(logits - local_max[:, None]), axis=1)
    stats = lax.all_gather(jnp.stack([local_max, local_total, taught]), "expert")
    highest = jnp.max(stats[:, 0], axis=0)
    totals = jnp.sum(stats[:, 1] * jnp.exp(stats[:, 0] - highest[None]), axis=0)
    picked_sum = jnp.sum(stats[:, 2], axis=0)
    log_total = highest + jnp.log(totals)
    entropy = jnp.sum(teacher_probs * jnp.log(teacher_probs), axis=1)
    terms = 2.0 * log_total - picked_sum + entropy
    loss_part = (
        jnp.sum(lax.dynamic_slice_in_dim(terms, my_index * loss_local, loss_local, 0)) / loss_count
    )
    soft = jnp.exp(logits - log_total[:, None])
    logit_grad = ((2.0 * soft - taken) / loss_count).astype(jnp.bfloat16)
    embed_head = jnp.einsum(
        "gv,gd->vd", logit_grad, group_final, preferred_element_type=jnp.float32
    ).astype(jnp.bfloat16)
    embed_head, head_grad = lax.optimization_barrier((embed_head, logit_grad))
    embed_sum = lax.psum_scatter(embed_head, "dp", scatter_dimension=1, tiled=True)
    final_parts = jnp.dot(head_grad, table_low, preferred_element_type=jnp.float32)
    final_grad = sum(
        swap(
            lax.dynamic_slice_in_dim(
                final_parts, partner_of(my_index, k, members) * loss_local, loss_local, 0
            ),
            k,
            members,
        )
        for k in range(members)
    )
    final_full = jnp.dot(
        place_hits.astype(jnp.float32).T, final_grad, precision=highest_precision
    )
    grad_two, gain_three = norm_backward(normal_three, factor_three, gain_rows[2], final_full)
    gate_grad = jnp.stack([jnp.sum(grad_two * part, axis=1) for part in picked], axis=1)
    chosen_grad = gating * (gate_grad - jnp.sum(gating * gate_grad, axis=1, keepdims=True))
    route_grad = jnp.sum(chosen_grad[:, :, None] * route_hits, axis=1)
    router_grad = jnp.dot(route_grad.T, moe_float, precision=highest_precision)
    moe_grad = jnp.dot(route_grad, router, precision=highest_precision)
    outgoing_grad = sum(
        jnp.einsum(
            "tr,td->rd",
            picks[j],
            (gating[:, j][:, None] * grad_two).astype(jnp.bfloat16),
            preferred_element_type=jnp.float32,
        )
        for j in range(TOP)
    ).astype(jnp.bfloat16)
    arrived_grad = (
        exchanged(outgoing_grad)
        .reshape(members, local_experts, capacity, width)
        .transpose(1, 0, 2, 3)
        .reshape(local_experts, members * capacity, width)
    )
    out_grad = jnp.einsum(
        "ecf,ecd->efd", activated, arrived_grad, preferred_element_type=jnp.float32
    )
    activated_grad = jnp.einsum(
        "ecd,efd->ecf", arrived_grad, out_low, preferred_element_type=jnp.float32
    )
    gelu_pull = jax.vjp(lambda inner: jax.nn.gelu(inner, approximate=True), expert_hidden)[1]
    hidden_grad = gelu_pull(activated_grad)[0].astype(jnp.bfloat16)
    in_grad = jnp.einsum("ecd,ecf->edf", arrived, hidden_grad, preferred_element_type=jnp.float32)
    rows_grad = jnp.einsum("ecf,edf->ecd", hidden_grad, in_low, preferred_element_type=jnp.float32)
    back_rows = sent_back(rows_grad.astype(jnp.bfloat16))
    back_rows, out_grad, in_grad, embed_sum = lax.optimization_barrier(
        (back_rows, out_grad.astype(jnp.bfloat16), in_grad.astype(jnp.bfloat16), embed_sum)
    )
    out_sum = lax.psum_scatter(out_grad, "dp", scatter_dimension=1, tiled=True)
    in_sum = lax.psum_scatter(in_grad, "dp", scatter_dimension=1, tiled=True)
    moe_grad = moe_grad + jnp.dot(any_pick, back_rows, preferred_element_type=jnp.float32)
    grad_part, gain_two = norm_backward(normal_two, factor_two, gain_rows[1], moe_grad)
    grad_one = grad_two + grad_part
    attn_grad = grad_one.astype(jnp.bfloat16)
    out_weight_grad = jnp.einsum("tc,td->cd", mixed, attn_grad, preferred_element_type=jnp.float32)
    mixed_grad = jnp.einsum(
        "td,cd->tc", attn_grad, dense_low[3], preferred_element_type=jnp.float32
    )
    mixed_grad = mixed_grad.astype(jnp.bfloat16).reshape(local_rows, head_count, HEAD)

    def backward_block(carry, inputs):
        keys_grad, values_grad = carry
        block_index, log_block = inputs
        scores, query_block, key_block, first_row = block_scores(
            query, keys, seg_ids, block_index, length, block_rows, scaling
        )
        soft_block = jnp.exp(scores - log_block[..., None])
        value_part = jnp.einsum(
            "hqk,qhd->khd",
            soft_block.astype(jnp.bfloat16),
            mixed_grad,
            preferred_element_type=jnp.float32,
        )
        weight_grad = jnp.einsum(
            "qhd,khd->hqk", mixed_grad, values, preferred_element_type=jnp.float32
        )
        score_grad = soft_block * (
            weight_grad - jnp.sum(soft_block * weight_grad, axis=-1, keepdims=True)
        )
        score_grad = score_grad.astype(jnp.bfloat16)
        query_part = (
            jnp.einsum("hqk,khd->qhd", score_grad, key_block, preferred_element_type=jnp.float32)
            * scaling
        )
        key_part = (
            jnp.einsum("hqk,qhd->khd", score_grad, query_block, preferred_element_type=jnp.float32)
            * scaling
        )
        keys_grad = keys_grad + key_part
        values_grad = values_grad + value_part
        return ((keys_grad, values_grad), query_part)

    zero_grad = jnp.zeros((local_rows, head_count, HEAD), jnp.float32)
    (keys_grad, values_grad), query_parts = lax.scan(
        backward_block, (zero_grad, zero_grad), (jnp.arange(block_count), log_totals)
    )
    projected_grad = jnp.stack(
        [
            query_parts.reshape(local_rows, width),
            keys_grad.reshape(local_rows, width),
            values_grad.reshape(local_rows, width),
        ]
    ).astype(jnp.bfloat16)
    qkv_grad = jnp.einsum(
        "td,jte->jde", attn_in, projected_grad, preferred_element_type=jnp.float32
    )
    attn_in_grad = jnp.einsum(
        "jte,jde->td", projected_grad, dense_low[:3], preferred_element_type=jnp.float32
    )
    grad_part, gain_one = norm_backward(normal_one, factor_one, gain_rows[0], attn_in_grad)
    stream_grad = (grad_one + grad_part).astype(jnp.bfloat16)
    attention_grad = jnp.concatenate([qkv_grad, out_weight_grad[None]], axis=0)
    small_grad = jnp.concatenate([jnp.stack([gain_one, gain_two, gain_three]), router_grad], axis=0)
    dense_grads = (
        attention_grad.reshape(attention.shape[0], replicas, share, width)
        .transpose(1, 0, 2, 3)
        .reshape(replicas, members, chunk, width)
        .astype(jnp.bfloat16)
    )
    stream_grad, dense_grads = lax.optimization_barrier((stream_grad, dense_grads))
    column_grad = lax.all_to_all(stream_grad, "dp", split_axis=1, concat_axis=0, tiled=True)
    column_grads = shared(column_grad.T, members)
    small_grads = small_grad.reshape(-1, replicas, share).transpose(1, 0, 2).reshape(replicas, -1)
    small_grads = jnp.concatenate(
        [
            small_grads,
            jnp.full((replicas, 1), loss_part),
            jnp.zeros((replicas, small_rows * width - small_params.size - 1), jnp.float32),
        ],
        axis=1,
    ).reshape(replicas, small_rows, width)

    def spread(values):
        return jnp.concatenate([part.astype(jnp.bfloat16) for part in in_thirds(values)], axis=1)

    def joined(values):
        parts = values.reshape(values.shape[0], -1, small_rows, width).astype(jnp.float32)
        return jnp.sum(parts, axis=1)

    def packed(dense, small):
        return jnp.concatenate([dense.astype(jnp.bfloat16), spread(small)], axis=1)

    def of_core(values, which):
        values = values.reshape((levels, 2) + values.shape[1:])
        return lax.dynamic_index_in_dim(values, which, 1, keepdims=False)

    dense_sum = of_core(dense_grads, core).astype(jnp.float32) + dp_swap(
        of_core(dense_grads, 1 - core), 1, replicas
    ).astype(jnp.float32)
    small_sum = of_core(small_grads, core) + joined(
        dp_swap(spread(of_core(small_grads, 1 - core)), 1, replicas)
    )
    received = [
        swap(
            packed(
                lax.dynamic_index_in_dim(
                    dense_sum, partner_of(my_index, k, members), 1, keepdims=False
                ),
                small_sum,
            ),
            k,
            members,
        )
        for k in range(members)
    ]
    token_rows = [
        lax.dynamic_index_in_dim(
            all_ids, partner_of(my_index, k, members), 1, keepdims=False
        ).reshape(-1)
        - my_index * vocab_rows
        for k in range(members)
    ]
    column_grads[1], out_sum = lax.optimization_barrier((column_grads[1], out_sum))
    third_out = nesterov_update(
        expert_out,
        expert_out_moment,
        expert_out_average,
        out_sum.astype(jnp.float32),
        RATE_TABLE[2] * loss_count**0.5,
    )
    half = members // 2
    stream_sum = add_rows(token_rows[:half], column_grads[:half], vocab_rows, None)
    received, stream_sum = lax.optimization_barrier((received, stream_sum))
    dense_sum = sum(part[:, :chunk].astype(jnp.float32) for part in received)
    small_sum = sum(joined(part[:, chunk:]) for part in received)
    message = packed(dense_sum, small_sum)
    summed = lax.dynamic_index_in_dim(dense_sum, level, 0, keepdims=False)
    small_sum = lax.dynamic_index_in_dim(small_sum, level, 0)
    for k in range(1, levels):
        part = dp_swap(lax.dynamic_index_in_dim(message, level ^ k, 0), 2 * k, replicas)
        summed = summed + part[0, :chunk].astype(jnp.float32)
        small_sum = small_sum + joined(part[:, chunk:])
    small_sum = small_sum.reshape(-1)
    column_grads[-1], third_out, summed = lax.optimization_barrier(
        (column_grads[-1], third_out, summed)
    )
    stream_sum = add_rows(token_rows[half:], column_grads[half:], vocab_rows, stream_sum)
    stream_sum, in_sum = lax.optimization_barrier((stream_sum, in_sum))
    embed_sum = embed_sum.astype(jnp.float32) + stream_sum.T
    in_sum = in_sum.astype(jnp.float32)
    loss_value = small_sum[small_params.size]
    small_sum = small_sum[: small_params.size].reshape(small_params.shape[0], share)
    attention_sum = in_order(shared(summed, members), my_index)
    attention_sum = attention_sum.reshape(attention.shape[0], share, width)
    rate_base = loss_count**0.5
    first_out = nesterov_update(
        attention, attention_moment, attention_average, attention_sum, RATE_TABLE[0] * rate_base
    )
    second_out = nesterov_update(
        expert_in, expert_in_moment, expert_in_average, in_sum, RATE_TABLE[1] * rate_base
    )
    fourth_out = nesterov_update(
        embedding, embedding_moment, embedding_average, embed_sum, RATE_TABLE[3] * rate_base
    )
    fifth_out = nesterov_update(
        small_params, small_moment, small_average, small_sum, RATE_TABLE[4] * rate_base
    )
    return (loss_value,) + first_out + second_out + third_out + fourth_out + fifth_out


def solution(mesh):
    return jax.shard_map(
        shards,
        mesh=mesh,
        in_specs=(
            P("dp", None),
            P(("dp", "expert"), None),
            P("dp", None, None),
            P(("dp", "expert")),
            P("dp"),
            P("dp", None),
            P("dp", None),
            P(None, "dp", None),
            P(None, "dp", None),
            P(None, "dp", None),
            P("expert", "dp", None),
            P("expert", "dp", None),
            P("expert", "dp", None),
            P("expert", "dp", None),
            P("expert", "dp", None),
            P("expert", "dp", None),
            P("expert", "dp"),
            P("expert", "dp"),
            P("expert", "dp"),
            P(None, "dp"),
            P(None, "dp"),
            P(None, "dp"),
        ),
        out_specs=(
            P(),
            P(None, "dp", None),
            P(None, "dp", None),
            P(None, "dp", None),
            P(None, "dp", None),
            P("expert", "dp", None),
            P("expert", "dp", None),
            P("expert", "dp", None),
            P("expert", "dp", None),
            P("expert", "dp", None),
            P("expert", "dp", None),
            P("expert", "dp", None),
            P("expert", "dp", None),
            P("expert", "dp"),
            P("expert", "dp"),
            P("expert", "dp"),
            P("expert", "dp"),
            P(None, "dp"),
            P(None, "dp"),
            P(None, "dp"),
            P(None, "dp"),
        ),
        check_vma=False,
    )
```

```python
import functools
import math

import jax
import jax.numpy as jnp
from jax import lax
from jax.experimental import pallas as pl
from jax.experimental.pallas import tpu as pltpu
from jax.sharding import PartitionSpec as P

HEAD = 64
TOP = 2
STEP = 7


EPSILON = 1e-06
MOMENTUM = 0.9
RATE_TABLE = (0.1, 0.3, 0.01, 0.05, 0.05)
MASKED_SCORE = -1e30


def partner_order(members):
    if members & (members - 1) == 0:
        return [[(i, i ^ k) for i in range(members)] for k in range(members)]
    return [[(i, (k - i) % members) for i in range(members)] for k in range(members)]


def partner_of(me, k, members):
    return me ^ k if members & (members - 1) == 0 else (k - me) % members


def swap(value, k, members):
    return value if k == 0 else lax.ppermute(value, "expert", partner_order(members)[k])


def dp_swap(value, k, replicas):
    return lax.ppermute(value, "dp", [(i, i ^ k) for i in range(replicas)]) if k else value


def in_order(parts, me):
    members = len(parts)
    stacked = jnp.stack(parts)
    return jnp.stack(
        [
            lax.dynamic_index_in_dim(stacked, partner_of(me, k, members), 0, keepdims=False)
            for k in range(members)
        ]
    )


def shared(value, members):
    return [swap(value, k, members) for k in range(members)]


def normal_parts(stream):
    factor = lax.rsqrt(jnp.mean(stream * stream, axis=-1, keepdims=True) + EPSILON)
    return (stream * factor, factor)


def norm_backward(normal, factor, gain, grad):
    gain_grad = jnp.sum(grad * normal, axis=0)
    normal_grad = grad * gain
    inner = jnp.mean(normal_grad * normal, axis=-1, keepdims=True)
    return (factor * (normal_grad - normal * inner), gain_grad)


def slot_table(block_routes, experts):
    flat = block_routes.reshape(-1)
    hits = (flat[:, None] == jnp.arange(experts, dtype=jnp.int32)[None, :]).astype(jnp.int32)
    place = jnp.arange(flat.shape[0], dtype=jnp.int32)
    earlier = (place[None, :] < place[:, None]).astype(jnp.bfloat16)
    before = jnp.dot(earlier, hits.astype(jnp.bfloat16), preferred_element_type=jnp.float32)
    return jnp.sum(before.astype(jnp.int32) * hits, axis=1).reshape(block_routes.shape)


def in_thirds(values):
    parts = []
    for _ in range(3):
        part = lax.reduce_precision(values, 8, 7)
        parts.append(part)
        values = values - part
    return parts


def label_weights(ids, weights, vocab_rows):
    lanes = 128
    tiles = (vocab_rows + lanes - 1) // lanes
    parts = in_thirds(weights)
    high = jnp.arange(tiles, dtype=jnp.int32)
    low = jnp.arange(lanes, dtype=jnp.int32)
    high_hits = (ids >> 7)[:, :, None] == high[None, None, :]
    rows = jnp.concatenate(
        [jnp.where(high_hits, part[:, :, None], 0.0).astype(jnp.bfloat16) for part in parts], axis=1
    )
    columns = ((ids & (lanes - 1))[:, :, None] == low[None, None, :]).astype(jnp.bfloat16)
    columns = jnp.concatenate([columns] * len(parts), axis=1)
    spread = jnp.einsum("pih,pil->phl", rows, columns, preferred_element_type=jnp.float32)
    return spread.reshape(ids.shape[0], tiles * lanes)[:, :vocab_rows]


LANES = 128
WAYS = 4
GRID_ROWS = 32768
VMEM_LIMIT = 56 * 2**20


def add_rows_kernel(count_ref, row_ref, source_ref, *refs):
    pieces = len(refs) - 2 - WAYS
    grad_refs, out_ref, grads, sums = refs[:pieces], refs[pieces], refs[pieces + 1], refs[-WAYS:]
    start_ref = None
    if grad_refs[-1].dtype == jnp.float32:
        start_ref, grad_refs = grad_refs[-1], grad_refs[:-1]
    width, piece = grad_refs[0].shape
    pad = jnp.zeros((LANES - width, LANES), jnp.float32)
    for k, grad_ref in enumerate(grad_refs):

        def turn(i, _, k=k, grad_ref=grad_ref):
            lanes = pl.ds(pl.multiple_of(i * LANES, LANES), LANES)
            tile = jnp.concatenate([grad_ref[:, lanes].astype(jnp.float32), pad], axis=0)
            grads[pl.ds(pl.multiple_of(k * piece + i * LANES, LANES), LANES), :] = tile.T
            return 0

        lax.fori_loop(0, piece // LANES, turn, 0)
    step = 64
    for total in sums:

        def clear(i, _, total=total):
            total[pl.ds(pl.multiple_of(i * step, step), step), :] = jnp.zeros(
                (step, LANES), jnp.float32
            )
            return 0

        lax.fori_loop(0, total.shape[0] // step, clear, 0)

    def one_block(b, _):
        def one_step(i, _):
            for w in range(WAYS):
                row = row_ref[b, i * WAYS + w]
                source = source_ref[b, i * WAYS + w]
                sums[w][pl.ds(row, 1), :] += grads[pl.ds(source, 1), :]
            return 0

        return lax.fori_loop(0, count_ref[b], one_step, 0)

    lax.fori_loop(0, row_ref.shape[0], one_block, 0)

    def finish(i, _):
        place = pl.ds(pl.multiple_of(i * LANES, LANES), LANES)
        total = sum(part[place, :] for part in sums)
        if start_ref is None:
            out_ref[place, :] = total
        else:
            out_ref[:, place] = (total + start_ref[place, :]).T[:width]
        return 0

    lax.fori_loop(0, sums[0].shape[0] // LANES, finish, 0)


def attend_kernel(scaling, q_ref, k_ref, v_ref, row_ref, column_ref, out_ref):
    length = q_ref.shape[0]
    rows = math.gcd(length, LANES)
    half = lax.broadcasted_iota(jnp.int32, (1, LANES), 1) // HEAD
    across = (((1,), (1,)), ((), ()))
    for block in range(length // rows):
        mine, seen = slice(block * rows, (block + 1) * rows), slice(0, (block + 1) * rows)
        keys, values = k_ref[seen, :], v_ref[seen, :]
        mixed = jnp.zeros((rows, LANES), jnp.float32)
        for part in range(LANES // HEAD):
            chosen = (half == part).astype(jnp.float32)
            query = q_ref[mine, :] * chosen.astype(jnp.bfloat16)
            scores = lax.dot_general(query, keys, across, preferred_element_type=jnp.float32)
            scores = scores * scaling
            row_place = lax.broadcasted_iota(jnp.int32, scores.shape, 0) + block * rows
            column_place = lax.broadcasted_iota(jnp.int32, scores.shape, 1)
            allowed = (column_place <= row_place) & (row_ref[mine, :] == column_ref[:, seen])
            scores = jnp.where(allowed, scores, MASKED_SCORE)
            powers = jnp.exp(scores - jnp.max(scores, axis=1, keepdims=True))
            soft = (powers / jnp.sum(powers, axis=1, keepdims=True)).astype(jnp.bfloat16)
            mixed += chosen * jnp.dot(soft, values, preferred_element_type=jnp.float32)
        out_ref[mine, :] = mixed.astype(jnp.bfloat16)


def attend(projected, seg_ids, sequences, scaling):
    _, count, width = projected.shape
    length = count // sequences

    def of(j):
        return pl.BlockSpec((None, length, LANES), lambda s, h: (j, s, h))

    return pl.pallas_call(
        functools.partial(attend_kernel, scaling),
        grid=(sequences, width // LANES),
        out_shape=jax.ShapeDtypeStruct((count, width), jnp.bfloat16),
        in_specs=[
            of(0),
            of(1),
            of(2),
            pl.BlockSpec((length, 1), lambda s, h: (s, 0)),
            pl.BlockSpec((1, length), lambda s, h: (0, s)),
        ],
        out_specs=pl.BlockSpec((length, LANES), lambda s, h: (s, h)),
        compiler_params=pltpu.CompilerParams(vmem_limit_bytes=VMEM_LIMIT),
        cost_estimate=pl.CostEstimate(
            flops=16 * count * length * width, bytes_accessed=8 * count * width, transcendentals=0
        ),
    )(projected, projected, projected, seg_ids[:, None], seg_ids[None, :])


def attend_back_kernel(scaling, q_ref, k_ref, v_ref, grad_ref, row_ref, column_ref, out_ref):
    length = q_ref.shape[0]
    rows = math.gcd(length, LANES)
    half = lax.broadcasted_iota(jnp.int32, (1, LANES), 1) // HEAD
    across = (((1,), (1,)), ((), ()))
    down = (((0,), (0,)), ((), ()))

    def product(a, b, dims):
        return lax.dot_general(a, b, dims, preferred_element_type=jnp.float32)

    def put(slot, place, values, first):
        if first:
            out_ref[slot, place, :] = values
        else:
            out_ref[slot, place, :] += values

    for part in range(LANES // HEAD):
        chosen = (half == part).astype(jnp.float32)
        only = chosen.astype(jnp.bfloat16)
        for block in range(length // rows):
            mine, seen = slice(block * rows, (block + 1) * rows), slice(0, (block + 1) * rows)
            fresh = part == 0
            query = q_ref[mine, :] * only
            grad = grad_ref[mine, :] * only
            keys, values = k_ref[seen, :], v_ref[seen, :]
            scores = product(query, keys, across) * scaling
            row_place = lax.broadcasted_iota(jnp.int32, scores.shape, 0) + block * rows
            column_place = lax.broadcasted_iota(jnp.int32, scores.shape, 1)
            allowed = (column_place <= row_place) & (row_ref[mine, :] == column_ref[:, seen])
            scores = jnp.where(allowed, scores, MASKED_SCORE)
            powers = jnp.exp(scores - jnp.max(scores, axis=1, keepdims=True))
            soft = powers / jnp.sum(powers, axis=1, keepdims=True)
            weight_grad = product(grad, values, across)
            score_grad = soft * (
                weight_grad - jnp.sum(soft * weight_grad, axis=1, keepdims=True)
            )
            score_grad = score_grad.astype(jnp.bfloat16)
            put(0, mine, product(score_grad, keys, (((1,), (0,)), ((), ()))) * (scaling * chosen), fresh)
            key_grad = product(score_grad, query, down) * scaling
            value_grad = product(soft.astype(jnp.bfloat16), grad, down)
            if fresh:
                key_new = slice(block * rows, (block + 1) * rows)
                if block:
                    old = slice(0, block * rows)
                    put(1, old, key_grad[: block * rows], False)
                    put(2, old, value_grad[: block * rows], False)
                put(1, key_new, key_grad[block * rows :], True)
                put(2, key_new, value_grad[block * rows :], True)
            else:
                put(1, seen, key_grad, False)
                put(2, seen, value_grad, False)


def attend_back(projected, grad, seg_ids, sequences, scaling):
    _, count, width = projected.shape
    length = count // sequences
    head_block = pl.BlockSpec((length, LANES), lambda s, h: (s, h))

    def of(j):
        return pl.BlockSpec((None, length, LANES), lambda s, h: (j, s, h))

    return pl.pallas_call(
        functools.partial(attend_back_kernel, scaling),
        grid=(sequences, width // LANES),
        out_shape=jax.ShapeDtypeStruct((3, count, width), jnp.float32),
        in_specs=[
            of(0),
            of(1),
            of(2),
            head_block,
            pl.BlockSpec((length, 1), lambda s, h: (s, 0)),
            pl.BlockSpec((1, length), lambda s, h: (0, s)),
        ],
        out_specs=pl.BlockSpec((3, length, LANES), lambda s, h: (0, s, h)),
        compiler_params=pltpu.CompilerParams(vmem_limit_bytes=VMEM_LIMIT),
        cost_estimate=pl.CostEstimate(
            flops=40 * count * length * width, bytes_accessed=20 * count * width, transcendentals=0
        ),
    )(projected, projected, projected, grad, seg_ids[:, None], seg_ids[None, :])


def row_lists(local_ids, vocab_rows, offset):
    ids = local_ids.reshape(-1, LANES)
    inside = (ids >= 0) & (ids < vocab_rows)
    place = jnp.arange(LANES, dtype=jnp.int32)
    earlier = (place[:, None] < place[None, :]).astype(jnp.bfloat16)
    before = jnp.dot(inside.astype(jnp.bfloat16), earlier, preferred_element_type=jnp.float32)
    chosen = inside[:, :, None] & (before.astype(jnp.int32)[:, :, None] == place[None, None, :])
    filled = jnp.sum(chosen.astype(jnp.int32), axis=1)
    rows = jnp.sum(jnp.where(chosen, ids[:, :, None], 0), axis=1)
    rows = jnp.where(filled > 0, rows, vocab_rows)
    origin = jnp.sum(jnp.where(chosen, place[None, :, None], 0), axis=1)
    origin = origin + offset + jnp.arange(ids.shape[0], dtype=jnp.int32)[:, None] * LANES
    counts = (jnp.sum(inside.astype(jnp.int32), axis=1) + WAYS - 1) // WAYS
    return counts, rows, origin


def add_rows(local_ids, grads, vocab_rows, start):
    width, piece = grads[0].shape
    if piece * len(grads) * 2 > GRID_ROWS or width > LANES or piece % LANES:
        vocab_iota = jnp.arange(vocab_rows, dtype=jnp.int32)
        total = jnp.zeros((width, vocab_rows), jnp.float32) if start is None else start
        for ids, part in zip(local_ids, grads):
            hits = (ids[:, None] == vocab_iota[None, :]).astype(jnp.bfloat16)
            total = total + jnp.dot(part, hits, preferred_element_type=jnp.float32)
        return total
    lists = [row_lists(ids, vocab_rows, k * piece) for k, ids in enumerate(local_ids)]
    lists = [jnp.concatenate(parts, axis=0) for parts in zip(*lists)]
    smem = pl.BlockSpec(memory_space=pltpu.SMEM)
    vmem = pl.BlockSpec(memory_space=pltpu.VMEM)
    padded_rows = -(-(vocab_rows + 1) // LANES) * LANES
    extra = [] if start is None else [start]
    shape = (padded_rows, LANES) if start is None else (width, padded_rows)
    summed = pl.pallas_call(
        add_rows_kernel,
        out_shape=jax.ShapeDtypeStruct(shape, jnp.float32),
        in_specs=[smem] * 3 + [vmem] * (len(grads) + len(extra)),
        out_specs=vmem,
        scratch_shapes=[pltpu.VMEM((len(grads) * piece, LANES), jnp.float32)]
        + [pltpu.VMEM((padded_rows, LANES), jnp.float32) for _ in range(WAYS)],
        compiler_params=pltpu.CompilerParams(vmem_limit_bytes=VMEM_LIMIT),
        cost_estimate=pl.CostEstimate(
            flops=len(grads) * piece * LANES * 8,
            bytes_accessed=4 * LANES * (2 * len(grads) * piece + 3 * WAYS * padded_rows) * 4,
            transcendentals=0,
        ),
    )(*lists, *grads, *extra)
    return summed if start is None else summed[:, :vocab_rows]


def nesterov_update(master, moment, average, grad, rate):
    moment_next = MOMENTUM * moment + grad
    master_next = master - rate * (grad + MOMENTUM * moment_next)
    average_next = average + (master_next - average) / (STEP + 1)
    return (master_next, moment_next, average_next, master_next.astype(jnp.bfloat16))


def shards(
    token_ids,
    segments,
    routes,
    positions,
    targets,
    teacher_ids,
    teacher_probs,
    attention,
    attention_moment,
    attention_average,
    expert_in,
    expert_in_moment,
    expert_in_average,
    expert_out,
    expert_out_moment,
    expert_out_average,
    embedding,
    embedding_moment,
    embedding_average,
    small_params,
    small_moment,
    small_average,
):
    members = lax.axis_size("expert")
    replicas = lax.axis_size("dp")
    my_index = lax.axis_index("expert")
    length = segments.shape[1]
    local_rows = segments.shape[0] * length
    width = attention.shape[2]
    local_experts = expert_in.shape[0]
    experts = local_experts * members
    vocab_rows = embedding.shape[0]
    capacity = max(2, 3 * local_rows * TOP // (2 * experts))
    loss_local = positions.shape[0]
    loss_count = loss_local * members * replicas
    scaling = HEAD ** (-0.5)
    highest_precision = lax.Precision.HIGHEST
    share = width // replicas
    chunk = attention.shape[0] * share // members
    small_rows = small_params.size // width + 1
    small_flat = jnp.pad(
        small_params.reshape(-1), (0, small_rows * width - small_params.size)
    ).reshape(small_rows, width)
    dense_part = lax.dynamic_slice_in_dim(
        attention.reshape(attention.shape[0] * share, width), my_index * chunk, chunk, 0
    )
    in_low, out_low, table_low = (
        lax.all_gather(expert_in.astype(jnp.bfloat16), "dp", axis=1, tiled=True),
        lax.all_gather(expert_out.astype(jnp.bfloat16), "dp", axis=1, tiled=True),
        lax.all_gather(embedding.astype(jnp.bfloat16), "dp", axis=1, tiled=True),
    )
    core = lax.axis_index("dp") & 1
    level = lax.axis_index("dp") >> 1
    levels = replicas // 2

    def by_core(value, axis):
        other = dp_swap(value, 1, replicas)
        first = jnp.where(core == 0, value, other)
        return jnp.stack([first, jnp.where(core == 0, other, value)], axis=axis)

    group_ids = token_ids.reshape(-1)
    own_routes = lax.dynamic_slice_in_dim(
        routes.reshape(members * local_rows, TOP), my_index * local_rows, local_rows, 0
    )
    target_local = targets - my_index * vocab_rows
    teacher_local = teacher_ids - my_index * vocab_rows
    taken = label_weights(
        jnp.concatenate([teacher_local, target_local[:, None]], axis=1),
        jnp.concatenate([teacher_probs, jnp.ones_like(teacher_probs[:, :1])], axis=1),
        vocab_rows,
    )
    rows_parts = shared(embedding.astype(jnp.bfloat16), members)
    id_rows = -(-2 * group_ids.shape[0] // width)
    digits = jnp.concatenate([group_ids >> 8, group_ids & 255])
    digits = jnp.pad(digits, (0, id_rows * width - digits.shape[0])).reshape(id_rows, width)
    dense_part = jnp.concatenate([dense_part, small_flat], axis=0).astype(jnp.bfloat16)
    dense_part = jnp.concatenate([dense_part, digits.astype(jnp.bfloat16)], axis=0)
    dense_part, rows_parts[1] = lax.optimization_barrier((dense_part, rows_parts[1]))
    rows_parts[-1], taken = lax.optimization_barrier((rows_parts[-1], taken))
    dense_part = in_order([dp_swap(dense_part, 2 * k, replicas) for k in range(levels)], level)
    others = by_core(dense_part[:, chunk:], 1).reshape(replicas, small_rows + id_rows, width)
    small_low, digits = others[:, :small_rows], others[:, small_rows:].reshape(replicas, -1)
    digits = digits[:, : 2 * group_ids.shape[0]].astype(jnp.int32)
    digits = digits.reshape(replicas, 2, members, local_rows)
    all_ids = digits[:, 0] * 256 + digits[:, 1]
    column_ids = lax.dynamic_index_in_dim(all_ids, my_index, 1, keepdims=False).reshape(-1)
    small_low = small_low.reshape(replicas, small_rows * width)
    small_low = small_low[:, : small_params.size].reshape(replicas, small_params.shape[0], share)
    small_low = small_low.transpose(1, 0, 2).reshape(small_params.shape[0], width)
    gain_rows = small_low[:3].astype(jnp.float32)
    router = small_low[3:].astype(jnp.float32)
    rows_parts[-1], dense_part = lax.optimization_barrier(
        (rows_parts[-1], dense_part[:, :chunk])
    )
    rows_table = jnp.concatenate(rows_parts, axis=0)
    places = partner_of(my_index, column_ids // vocab_rows, members) * vocab_rows
    places = places + column_ids % vocab_rows
    stream_parts = jnp.take(rows_table, places, axis=0, mode="clip")
    dense_parts = shared(dense_part, members)
    stream_parts, dense_parts = lax.optimization_barrier((stream_parts, dense_parts))
    dense_low = by_core(in_order(dense_parts, my_index), 2)
    dense_low = (
        dense_low.reshape(members, replicas, chunk, width)
        .transpose(1, 0, 2, 3)
        .reshape(replicas, attention.shape[0], share, width)
        .transpose(1, 0, 2, 3)
        .reshape(attention.shape[0], width, width)
    )
    stream = lax.all_to_all(
        stream_parts, "dp", split_axis=0, concat_axis=1, tiled=True
    ).astype(jnp.float32)
    normal_one, factor_one = normal_parts(stream)
    attn_in = (normal_one * gain_rows[0]).astype(jnp.bfloat16)
    projected = jnp.einsum(
        "td,jde->jte", attn_in, dense_low[:3], preferred_element_type=jnp.float32
    ).astype(jnp.bfloat16)
    seg_ids = segments.reshape(-1)

    mixed = attend(projected, seg_ids, local_rows // length, scaling)
    hidden_one = stream + jnp.dot(mixed, dense_low[3], preferred_element_type=jnp.float32)
    normal_two, factor_two = normal_parts(hidden_one)
    moe_in = (normal_two * gain_rows[1]).astype(jnp.bfloat16)
    moe_float = moe_in.astype(jnp.float32)
    router_logits = jnp.dot(moe_float, router.T, precision=highest_precision)
    expert_ids = jnp.arange(experts, dtype=jnp.int32)
    route_hits = (own_routes[:, :, None] == expert_ids[None, None, :]).astype(jnp.float32)
    chosen = jnp.sum(router_logits[:, None, :] * route_hits, axis=2)
    gating = jnp.exp(chosen - jnp.max(chosen, axis=1, keepdims=True))
    gating = gating / jnp.sum(gating, axis=1, keepdims=True)
    slots = slot_table(own_routes, experts)
    block = local_experts * capacity
    landing = partner_of(my_index, own_routes // local_experts, members) * block
    landing = landing + own_routes % local_experts * capacity + slots
    landing_iota = jnp.arange(members * block, dtype=jnp.int32)
    picks = [
        (landing[:, j][:, None] == landing_iota[None, :]).astype(jnp.bfloat16) for j in range(TOP)
    ]
    any_pick = sum(picks)

    def exchanged(rows):
        parts = rows.reshape(members, block, rows.shape[1])
        return jnp.stack([swap(parts[k], k, members) for k in range(members)])

    outgoing = jnp.einsum("tr,td->rd", any_pick, moe_in, preferred_element_type=jnp.float32)
    arrived = exchanged(outgoing.astype(jnp.bfloat16))
    arrived = (
        arrived.reshape(members, local_experts, capacity, width)
        .transpose(1, 0, 2, 3)
        .reshape(local_experts, members * capacity, width)
    )

    def sent_back(rows):
        rows = rows.reshape(local_experts, members, capacity, width).transpose(1, 0, 2, 3)
        return exchanged(rows.reshape(members * block, width)).reshape(members * block, width)

    expert_hidden = jnp.einsum("ecd,edf->ecf", arrived, in_low, preferred_element_type=jnp.float32)
    activated = jax.nn.gelu(expert_hidden, approximate=True).astype(jnp.bfloat16)
    expert_result = jnp.einsum(
        "ecf,efd->ecd", activated, out_low, preferred_element_type=jnp.float32
    ).astype(jnp.bfloat16)
    returned = sent_back(expert_result)
    picked = [jnp.dot(pick, returned, preferred_element_type=jnp.float32) for pick in picks]
    hidden_two = hidden_one + sum(gating[:, j][:, None] * picked[j] for j in range(TOP))
    normal_three, factor_three = normal_parts(hidden_two)
    final = (normal_three * gain_rows[2]).astype(jnp.bfloat16)
    place_hits = positions[:, None] == jnp.arange(local_rows, dtype=jnp.int32)[None, :]
    final_rows = jnp.dot(
        place_hits.astype(jnp.bfloat16), final, preferred_element_type=jnp.float32
    ).astype(jnp.bfloat16)
    group_final = lax.all_gather(final_rows, "expert", axis=0, tiled=True)
    logits = jnp.einsum("gd,vd->gv", group_final, table_low, preferred_element_type=jnp.float32)
    taught = jnp.sum(taken * logits, axis=1)
    local_max = jnp.max(logits, axis=1)
    local_total = jnp.sum(jnp.exp(logits - local_max[:, None]), axis=1)
    stats = lax.all_gather(jnp.stack([local_max, local_total, taught]), "expert")
    highest = jnp.max(stats[:, 0], axis=0)
    totals = jnp.sum(stats[:, 1] * jnp.exp(stats[:, 0] - highest[None]), axis=0)
    picked_sum = jnp.sum(stats[:, 2], axis=0)
    log_total = highest + jnp.log(totals)
    entropy = jnp.sum(teacher_probs * jnp.log(teacher_probs), axis=1)
    terms = 2.0 * log_total - picked_sum + entropy
    loss_part = (
        jnp.sum(lax.dynamic_slice_in_dim(terms, my_index * loss_local, loss_local, 0)) / loss_count
    )
    soft = jnp.exp(logits - log_total[:, None])
    logit_grad = ((2.0 * soft - taken) / loss_count).astype(jnp.bfloat16)
    embed_head = jnp.einsum(
        "gv,gd->vd", logit_grad, group_final, preferred_element_type=jnp.float32
    ).astype(jnp.bfloat16)
    embed_head, head_grad = lax.optimization_barrier((embed_head, logit_grad))
    embed_sum = lax.psum_scatter(embed_head, "dp", scatter_dimension=1, tiled=True)
    final_parts = jnp.dot(head_grad, table_low, preferred_element_type=jnp.float32)
    final_grad = sum(
        swap(
            lax.dynamic_slice_in_dim(
                final_parts, partner_of(my_index, k, members) * loss_local, loss_local, 0
            ),
            k,
            members,
        )
        for k in range(members)
    )
    final_full = jnp.dot(
        place_hits.astype(jnp.float32).T, final_grad, precision=highest_precision
    )
    grad_two, gain_three = norm_backward(normal_three, factor_three, gain_rows[2], final_full)
    gate_grad = jnp.stack([jnp.sum(grad_two * part, axis=1) for part in picked], axis=1)
    chosen_grad = gating * (gate_grad - jnp.sum(gating * gate_grad, axis=1, keepdims=True))
    route_grad = jnp.sum(chosen_grad[:, :, None] * route_hits, axis=1)
    router_grad = jnp.dot(route_grad.T, moe_float, precision=highest_precision)
    moe_grad = jnp.dot(route_grad, router, precision=highest_precision)
    outgoing_grad = sum(
        jnp.einsum(
            "tr,td->rd",
            picks[j],
            (gating[:, j][:, None] * grad_two).astype(jnp.bfloat16),
            preferred_element_type=jnp.float32,
        )
        for j in range(TOP)
    ).astype(jnp.bfloat16)
    arrived_grad = (
        exchanged(outgoing_grad)
        .reshape(members, local_experts, capacity, width)
        .transpose(1, 0, 2, 3)
        .reshape(local_experts, members * capacity, width)
    )
    out_grad = jnp.einsum(
        "ecf,ecd->efd", activated, arrived_grad, preferred_element_type=jnp.float32
    )
    activated_grad = jnp.einsum(
        "ecd,efd->ecf", arrived_grad, out_low, preferred_element_type=jnp.float32
    )
    gelu_pull = jax.vjp(lambda inner: jax.nn.gelu(inner, approximate=True), expert_hidden)[1]
    hidden_grad = gelu_pull(activated_grad)[0].astype(jnp.bfloat16)
    in_grad = jnp.einsum("ecd,ecf->edf", arrived, hidden_grad, preferred_element_type=jnp.float32)
    rows_grad = jnp.einsum("ecf,edf->ecd", hidden_grad, in_low, preferred_element_type=jnp.float32)
    back_rows = sent_back(rows_grad.astype(jnp.bfloat16))
    back_rows, out_grad, in_grad, embed_sum = lax.optimization_barrier(
        (back_rows, out_grad.astype(jnp.bfloat16), in_grad.astype(jnp.bfloat16), embed_sum)
    )
    out_sum = lax.psum_scatter(out_grad, "dp", scatter_dimension=1, tiled=True)
    in_sum = lax.psum_scatter(in_grad, "dp", scatter_dimension=1, tiled=True)
    moe_grad = moe_grad + jnp.dot(any_pick, back_rows, preferred_element_type=jnp.float32)
    grad_part, gain_two = norm_backward(normal_two, factor_two, gain_rows[1], moe_grad)
    grad_one = grad_two + grad_part
    attn_grad = grad_one.astype(jnp.bfloat16)
    out_weight_grad = jnp.einsum("tc,td->cd", mixed, attn_grad, preferred_element_type=jnp.float32)
    mixed_grad = jnp.einsum(
        "td,cd->tc", attn_grad, dense_low[3], preferred_element_type=jnp.float32
    )
    mixed_grad = mixed_grad.astype(jnp.bfloat16)

    projected_grad = attend_back(
        projected, mixed_grad, seg_ids, local_rows // length, scaling
    ).astype(jnp.bfloat16)
    qkv_grad = jnp.einsum(
        "td,jte->jde", attn_in, projected_grad, preferred_element_type=jnp.float32
    )
    attn_in_grad = jnp.einsum(
        "jte,jde->td", projected_grad, dense_low[:3], preferred_element_type=jnp.float32
    )
    grad_part, gain_one = norm_backward(normal_one, factor_one, gain_rows[0], attn_in_grad)
    stream_grad = (grad_one + grad_part).astype(jnp.bfloat16)
    attention_grad = jnp.concatenate([qkv_grad, out_weight_grad[None]], axis=0)
    small_grad = jnp.concatenate([jnp.stack([gain_one, gain_two, gain_three]), router_grad], axis=0)
    dense_grads = (
        attention_grad.reshape(attention.shape[0], replicas, share, width)
        .transpose(1, 0, 2, 3)
        .reshape(replicas, members, chunk, width)
        .astype(jnp.bfloat16)
    )
    stream_grad, dense_grads = lax.optimization_barrier((stream_grad, dense_grads))
    column_grad = lax.all_to_all(stream_grad, "dp", split_axis=1, concat_axis=0, tiled=True)
    column_grads = shared(column_grad.T, members)
    small_grads = small_grad.reshape(-1, replicas, share).transpose(1, 0, 2).reshape(replicas, -1)
    small_grads = jnp.concatenate(
        [
            small_grads,
            jnp.full((replicas, 1), loss_part),
            jnp.zeros((replicas, small_rows * width - small_params.size - 1), jnp.float32),
        ],
        axis=1,
    ).reshape(replicas, small_rows, width)

    def spread(values):
        return jnp.concatenate([part.astype(jnp.bfloat16) for part in in_thirds(values)], axis=1)

    def joined(values):
        parts = values.reshape(values.shape[0], -1, small_rows, width).astype(jnp.float32)
        return jnp.sum(parts, axis=1)

    def packed(dense, small):
        return jnp.concatenate([dense.astype(jnp.bfloat16), spread(small)], axis=1)

    def of_core(values, which):
        values = values.reshape((levels, 2) + values.shape[1:])
        return lax.dynamic_index_in_dim(values, which, 1, keepdims=False)

    dense_sum = of_core(dense_grads, core).astype(jnp.float32) + dp_swap(
        of_core(dense_grads, 1 - core), 1, replicas
    ).astype(jnp.float32)
    small_sum = of_core(small_grads, core) + joined(
        dp_swap(spread(of_core(small_grads, 1 - core)), 1, replicas)
    )
    received = [
        swap(
            packed(
                lax.dynamic_index_in_dim(
                    dense_sum, partner_of(my_index, k, members), 1, keepdims=False
                ),
                small_sum,
            ),
            k,
            members,
        )
        for k in range(members)
    ]
    token_rows = [
        lax.dynamic_index_in_dim(
            all_ids, partner_of(my_index, k, members), 1, keepdims=False
        ).reshape(-1)
        - my_index * vocab_rows
        for k in range(members)
    ]
    column_grads[1], out_sum = lax.optimization_barrier((column_grads[1], out_sum))
    third_out = nesterov_update(
        expert_out,
        expert_out_moment,
        expert_out_average,
        out_sum.astype(jnp.float32),
        RATE_TABLE[2] * loss_count**0.5,
    )
    half = members // 2
    stream_sum = add_rows(token_rows[:half], column_grads[:half], vocab_rows, None)
    received, stream_sum = lax.optimization_barrier((received, stream_sum))
    dense_sum = sum(part[:, :chunk].astype(jnp.float32) for part in received)
    small_sum = sum(joined(part[:, chunk:]) for part in received)
    message = packed(dense_sum, small_sum)
    summed = lax.dynamic_index_in_dim(dense_sum, level, 0, keepdims=False)
    small_sum = lax.dynamic_index_in_dim(small_sum, level, 0)
    for k in range(1, levels):
        part = dp_swap(lax.dynamic_index_in_dim(message, level ^ k, 0), 2 * k, replicas)
        summed = summed + part[0, :chunk].astype(jnp.float32)
        small_sum = small_sum + joined(part[:, chunk:])
    small_sum = small_sum.reshape(-1)
    column_grads[-1], third_out, summed = lax.optimization_barrier(
        (column_grads[-1], third_out, summed)
    )
    stream_sum = add_rows(token_rows[half:], column_grads[half:], vocab_rows, stream_sum)
    embed_sum = embed_sum.astype(jnp.float32) + stream_sum.T
    loss_value = small_sum[small_params.size]
    small_sum = small_sum[: small_params.size].reshape(small_params.shape[0], share)
    attention_sum = in_order(shared(summed, members), my_index)
    attention_sum = attention_sum.reshape(attention.shape[0], share, width)
    rate_base = loss_count**0.5
    first_out = nesterov_update(
        attention, attention_moment, attention_average, attention_sum, RATE_TABLE[0] * rate_base
    )
    fourth_out = nesterov_update(
        embedding, embedding_moment, embedding_average, embed_sum, RATE_TABLE[3] * rate_base
    )
    fifth_out = nesterov_update(
        small_params, small_moment, small_average, small_sum, RATE_TABLE[4] * rate_base
    )
    first_out, fourth_out, fifth_out, in_sum = lax.optimization_barrier(
        (first_out, fourth_out, fifth_out, in_sum)
    )
    second_out = nesterov_update(
        expert_in, expert_in_moment, expert_in_average, in_sum.astype(jnp.float32), RATE_TABLE[1] * rate_base
    )
    return (loss_value,) + first_out + second_out + third_out + fourth_out + fifth_out


def solution(mesh):
    return jax.shard_map(
        shards,
        mesh=mesh,
        in_specs=(
            P("dp", None),
            P(("dp", "expert"), None),
            P("dp", None, None),
            P(("dp", "expert")),
            P("dp"),
            P("dp", None),
            P("dp", None),
            P(None, "dp", None),
            P(None, "dp", None),
            P(None, "dp", None),
            P("expert", "dp", None),
            P("expert", "dp", None),
            P("expert", "dp", None),
            P("expert", "dp", None),
            P("expert", "dp", None),
            P("expert", "dp", None),
            P("expert", "dp"),
            P("expert", "dp"),
            P("expert", "dp"),
            P(None, "dp"),
            P(None, "dp"),
            P(None, "dp"),
        ),
        out_specs=(
            P(),
            P(None, "dp", None),
            P(None, "dp", None),
            P(None, "dp", None),
            P(None, "dp", None),
            P("expert", "dp", None),
            P("expert", "dp", None),
            P("expert", "dp", None),
            P("expert", "dp", None),
            P("expert", "dp", None),
            P("expert", "dp", None),
            P("expert", "dp", None),
            P("expert", "dp", None),
            P("expert", "dp"),
            P("expert", "dp"),
            P("expert", "dp"),
            P("expert", "dp"),
            P(None, "dp"),
            P(None, "dp"),
            P(None, "dp"),
            P(None, "dp"),
        ),
        check_vma=False,
    )
```

```python
import functools
import math

import jax
import jax.numpy as jnp
from jax import lax
from jax.experimental import pallas as pl
from jax.experimental.pallas import tpu as pltpu
from jax.sharding import PartitionSpec as P

HEAD = 64
TOP = 2
STEP = 7


EPSILON = 1e-06
MOMENTUM = 0.9
RATE_TABLE = (0.1, 0.3, 0.01, 0.05, 0.05)
MASKED_SCORE = -1e30


def partner_order(members):
    if members & (members - 1) == 0:
        return [[(i, i ^ k) for i in range(members)] for k in range(members)]
    return [[(i, (k - i) % members) for i in range(members)] for k in range(members)]


def partner_of(me, k, members):
    return me ^ k if members & (members - 1) == 0 else (k - me) % members


def swap(value, k, members):
    return value if k == 0 else lax.ppermute(value, "expert", partner_order(members)[k])


def dp_swap(value, k, replicas):
    return lax.ppermute(value, "dp", [(i, i ^ k) for i in range(replicas)]) if k else value


def in_order(parts, me):
    members = len(parts)
    stacked = jnp.stack(parts)
    return jnp.stack(
        [
            lax.dynamic_index_in_dim(stacked, partner_of(me, k, members), 0, keepdims=False)
            for k in range(members)
        ]
    )


def shared(value, members):
    return [swap(value, k, members) for k in range(members)]


def normal_parts(stream):
    factor = lax.rsqrt(jnp.mean(stream * stream, axis=-1, keepdims=True) + EPSILON)
    return (stream * factor, factor)


def norm_backward(normal, factor, gain, grad):
    gain_grad = jnp.sum(grad * normal, axis=0)
    normal_grad = grad * gain
    inner = jnp.mean(normal_grad * normal, axis=-1, keepdims=True)
    return (factor * (normal_grad - normal * inner), gain_grad)


def slot_table(block_routes, experts):
    flat = block_routes.reshape(-1)
    hits = (flat[:, None] == jnp.arange(experts, dtype=jnp.int32)[None, :]).astype(jnp.int32)
    place = jnp.arange(flat.shape[0], dtype=jnp.int32)
    earlier = (place[None, :] < place[:, None]).astype(jnp.bfloat16)
    before = jnp.dot(earlier, hits.astype(jnp.bfloat16), preferred_element_type=jnp.float32)
    return jnp.sum(before.astype(jnp.int32) * hits, axis=1).reshape(block_routes.shape)


def in_thirds(values):
    parts = []
    for _ in range(3):
        part = lax.reduce_precision(values, 8, 7)
        parts.append(part)
        values = values - part
    return parts


def label_weights(ids, weights, vocab_rows):
    lanes = 128
    tiles = (vocab_rows + lanes - 1) // lanes
    parts = in_thirds(weights)
    high = jnp.arange(tiles, dtype=jnp.int32)
    low = jnp.arange(lanes, dtype=jnp.int32)
    high_hits = (ids >> 7)[:, :, None] == high[None, None, :]
    rows = jnp.concatenate(
        [jnp.where(high_hits, part[:, :, None], 0.0).astype(jnp.bfloat16) for part in parts], axis=1
    )
    columns = ((ids & (lanes - 1))[:, :, None] == low[None, None, :]).astype(jnp.bfloat16)
    columns = jnp.concatenate([columns] * len(parts), axis=1)
    spread = jnp.einsum("pih,pil->phl", rows, columns, preferred_element_type=jnp.float32)
    return spread.reshape(ids.shape[0], tiles * lanes)[:, :vocab_rows]


LANES = 128
WAYS = 4
GRID_ROWS = 32768
VMEM_LIMIT = 56 * 2**20


def add_rows_kernel(count_ref, row_ref, source_ref, *refs):
    pieces = len(refs) - 2 - WAYS
    grad_refs, out_ref, grads, sums = refs[:pieces], refs[pieces], refs[pieces + 1], refs[-WAYS:]
    start_ref = None
    if grad_refs[-1].dtype == jnp.float32:
        start_ref, grad_refs = grad_refs[-1], grad_refs[:-1]
    width, piece = grad_refs[0].shape
    pad = jnp.zeros((LANES - width, LANES), jnp.float32)
    for k, grad_ref in enumerate(grad_refs):

        def turn(i, _, k=k, grad_ref=grad_ref):
            lanes = pl.ds(pl.multiple_of(i * LANES, LANES), LANES)
            tile = jnp.concatenate([grad_ref[:, lanes].astype(jnp.float32), pad], axis=0)
            grads[pl.ds(pl.multiple_of(k * piece + i * LANES, LANES), LANES), :] = tile.T
            return 0

        lax.fori_loop(0, piece // LANES, turn, 0)
    step = 64
    for total in sums:

        def clear(i, _, total=total):
            total[pl.ds(pl.multiple_of(i * step, step), step), :] = jnp.zeros(
                (step, LANES), jnp.float32
            )
            return 0

        lax.fori_loop(0, total.shape[0] // step, clear, 0)

    def one_block(b, _):
        def one_step(i, _):
            for w in range(WAYS):
                row = row_ref[b, i * WAYS + w]
                source = source_ref[b, i * WAYS + w]
                sums[w][pl.ds(row, 1), :] += grads[pl.ds(source, 1), :]
            return 0

        return lax.fori_loop(0, count_ref[b], one_step, 0)

    lax.fori_loop(0, row_ref.shape[0], one_block, 0)

    def finish(i, _):
        place = pl.ds(pl.multiple_of(i * LANES, LANES), LANES)
        total = sum(part[place, :] for part in sums)
        if start_ref is None:
            out_ref[place, :] = total
        else:
            out_ref[:, place] = (total + start_ref[place, :]).T[:width]
        return 0

    lax.fori_loop(0, sums[0].shape[0] // LANES, finish, 0)


def attend_kernel(scaling, q_ref, k_ref, v_ref, row_ref, column_ref, out_ref):
    length = q_ref.shape[0]
    rows = math.gcd(length, LANES)
    half = lax.broadcasted_iota(jnp.int32, (1, LANES), 1) // HEAD
    across = (((1,), (1,)), ((), ()))
    for block in range(length // rows):
        mine, seen = slice(block * rows, (block + 1) * rows), slice(0, (block + 1) * rows)
        keys, values = k_ref[seen, :], v_ref[seen, :]
        mixed = jnp.zeros((rows, LANES), jnp.float32)
        for part in range(LANES // HEAD):
            chosen = (half == part).astype(jnp.float32)
            query = q_ref[mine, :] * chosen.astype(jnp.bfloat16)
            scores = lax.dot_general(query, keys, across, preferred_element_type=jnp.float32)
            scores = scores * scaling
            row_place = lax.broadcasted_iota(jnp.int32, scores.shape, 0) + block * rows
            column_place = lax.broadcasted_iota(jnp.int32, scores.shape, 1)
            allowed = (column_place <= row_place) & (row_ref[mine, :] == column_ref[:, seen])
            scores = jnp.where(allowed, scores, MASKED_SCORE)
            powers = jnp.exp(scores - jnp.max(scores, axis=1, keepdims=True))
            soft = (powers / jnp.sum(powers, axis=1, keepdims=True)).astype(jnp.bfloat16)
            mixed += chosen * jnp.dot(soft, values, preferred_element_type=jnp.float32)
        out_ref[mine, :] = mixed.astype(jnp.bfloat16)


def attend(projected, seg_ids, sequences, scaling):
    _, count, width = projected.shape
    length = count // sequences

    def of(j):
        return pl.BlockSpec((None, length, LANES), lambda s, h: (j, s, h))

    return pl.pallas_call(
        functools.partial(attend_kernel, scaling),
        grid=(sequences, width // LANES),
        out_shape=jax.ShapeDtypeStruct((count, width), jnp.bfloat16),
        in_specs=[
            of(0),
            of(1),
            of(2),
            pl.BlockSpec((length, 1), lambda s, h: (s, 0)),
            pl.BlockSpec((1, length), lambda s, h: (0, s)),
        ],
        out_specs=pl.BlockSpec((length, LANES), lambda s, h: (s, h)),
        compiler_params=pltpu.CompilerParams(vmem_limit_bytes=VMEM_LIMIT),
        cost_estimate=pl.CostEstimate(
            flops=16 * count * length * width, bytes_accessed=8 * count * width, transcendentals=0
        ),
    )(projected, projected, projected, seg_ids[:, None], seg_ids[None, :])


def attend_back_kernel(scaling, q_ref, k_ref, v_ref, grad_ref, row_ref, column_ref, out_ref):
    length = q_ref.shape[0]
    rows = math.gcd(length, LANES)
    half = lax.broadcasted_iota(jnp.int32, (1, LANES), 1) // HEAD
    across = (((1,), (1,)), ((), ()))
    down = (((0,), (0,)), ((), ()))

    def product(a, b, dims):
        return lax.dot_general(a, b, dims, preferred_element_type=jnp.float32)

    def put(slot, place, values, first):
        if first:
            out_ref[slot, place, :] = values
        else:
            out_ref[slot, place, :] += values

    for part in range(LANES // HEAD):
        chosen = (half == part).astype(jnp.float32)
        only = chosen.astype(jnp.bfloat16)
        for block in range(length // rows):
            mine, seen = slice(block * rows, (block + 1) * rows), slice(0, (block + 1) * rows)
            fresh = part == 0
            query = q_ref[mine, :] * only
            grad = grad_ref[mine, :] * only
            keys, values = k_ref[seen, :], v_ref[seen, :]
            scores = product(query, keys, across) * scaling
            row_place = lax.broadcasted_iota(jnp.int32, scores.shape, 0) + block * rows
            column_place = lax.broadcasted_iota(jnp.int32, scores.shape, 1)
            allowed = (column_place <= row_place) & (row_ref[mine, :] == column_ref[:, seen])
            scores = jnp.where(allowed, scores, MASKED_SCORE)
            powers = jnp.exp(scores - jnp.max(scores, axis=1, keepdims=True))
            soft = powers / jnp.sum(powers, axis=1, keepdims=True)
            weight_grad = product(grad, values, across)
            score_grad = soft * (
                weight_grad - jnp.sum(soft * weight_grad, axis=1, keepdims=True)
            )
            score_grad = score_grad.astype(jnp.bfloat16)
            put(0, mine, product(score_grad, keys, (((1,), (0,)), ((), ()))) * (scaling * chosen), fresh)
            key_grad = product(score_grad, query, down) * scaling
            value_grad = product(soft.astype(jnp.bfloat16), grad, down)
            if fresh:
                key_new = slice(block * rows, (block + 1) * rows)
                if block:
                    old = slice(0, block * rows)
                    put(1, old, key_grad[: block * rows], False)
                    put(2, old, value_grad[: block * rows], False)
                put(1, key_new, key_grad[block * rows :], True)
                put(2, key_new, value_grad[block * rows :], True)
            else:
                put(1, seen, key_grad, False)
                put(2, seen, value_grad, False)


def attend_back(projected, grad, seg_ids, sequences, scaling):
    _, count, width = projected.shape
    length = count // sequences
    head_block = pl.BlockSpec((length, LANES), lambda s, h: (s, h))

    def of(j):
        return pl.BlockSpec((None, length, LANES), lambda s, h: (j, s, h))

    return pl.pallas_call(
        functools.partial(attend_back_kernel, scaling),
        grid=(sequences, width // LANES),
        out_shape=jax.ShapeDtypeStruct((3, count, width), jnp.float32),
        in_specs=[
            of(0),
            of(1),
            of(2),
            head_block,
            pl.BlockSpec((length, 1), lambda s, h: (s, 0)),
            pl.BlockSpec((1, length), lambda s, h: (0, s)),
        ],
        out_specs=pl.BlockSpec((3, length, LANES), lambda s, h: (0, s, h)),
        compiler_params=pltpu.CompilerParams(vmem_limit_bytes=VMEM_LIMIT),
        cost_estimate=pl.CostEstimate(
            flops=40 * count * length * width, bytes_accessed=20 * count * width, transcendentals=0
        ),
    )(projected, projected, projected, grad, seg_ids[:, None], seg_ids[None, :])


def row_lists(local_ids, vocab_rows, offset):
    ids = local_ids.reshape(-1, LANES)
    inside = (ids >= 0) & (ids < vocab_rows)
    place = jnp.arange(LANES, dtype=jnp.int32)
    earlier = (place[:, None] < place[None, :]).astype(jnp.bfloat16)
    before = jnp.dot(inside.astype(jnp.bfloat16), earlier, preferred_element_type=jnp.float32)
    chosen = inside[:, :, None] & (before.astype(jnp.int32)[:, :, None] == place[None, None, :])
    filled = jnp.sum(chosen.astype(jnp.int32), axis=1)
    rows = jnp.sum(jnp.where(chosen, ids[:, :, None], 0), axis=1)
    rows = jnp.where(filled > 0, rows, vocab_rows)
    origin = jnp.sum(jnp.where(chosen, place[None, :, None], 0), axis=1)
    origin = origin + offset + jnp.arange(ids.shape[0], dtype=jnp.int32)[:, None] * LANES
    counts = (jnp.sum(inside.astype(jnp.int32), axis=1) + WAYS - 1) // WAYS
    return counts, rows, origin


def takes_kernel(pieces, piece, width):
    return piece * pieces * 2 <= GRID_ROWS and width <= LANES and piece % LANES == 0


def all_lists(local_ids, vocab_rows):
    lists = [row_lists(ids, vocab_rows, k * ids.shape[0]) for k, ids in enumerate(local_ids)]
    return tuple(jnp.concatenate(parts, axis=0) for parts in zip(*lists))


def add_rows(local_ids, lists, grads, vocab_rows, start):
    width, piece = grads[0].shape
    if not takes_kernel(len(grads), piece, width):
        vocab_iota = jnp.arange(vocab_rows, dtype=jnp.int32)
        total = jnp.zeros((width, vocab_rows), jnp.float32) if start is None else start
        for ids, part in zip(local_ids, grads):
            hits = (ids[:, None] == vocab_iota[None, :]).astype(jnp.bfloat16)
            total = total + jnp.dot(part, hits, preferred_element_type=jnp.float32)
        return total
    smem = pl.BlockSpec(memory_space=pltpu.SMEM)
    vmem = pl.BlockSpec(memory_space=pltpu.VMEM)
    padded_rows = -(-(vocab_rows + 1) // LANES) * LANES
    extra = [] if start is None else [start]
    shape = (padded_rows, LANES) if start is None else (width, padded_rows)
    summed = pl.pallas_call(
        add_rows_kernel,
        out_shape=jax.ShapeDtypeStruct(shape, jnp.float32),
        in_specs=[smem] * 3 + [vmem] * (len(grads) + len(extra)),
        out_specs=vmem,
        scratch_shapes=[pltpu.VMEM((len(grads) * piece, LANES), jnp.float32)]
        + [pltpu.VMEM((padded_rows, LANES), jnp.float32) for _ in range(WAYS)],
        compiler_params=pltpu.CompilerParams(vmem_limit_bytes=VMEM_LIMIT),
        cost_estimate=pl.CostEstimate(
            flops=len(grads) * piece * LANES * 8,
            bytes_accessed=4 * LANES * (2 * len(grads) * piece + 3 * WAYS * padded_rows) * 4,
            transcendentals=0,
        ),
    )(*lists, *grads, *extra)
    return summed if start is None else summed[:, :vocab_rows]


def nesterov_update(master, moment, average, grad, rate):
    moment_next = MOMENTUM * moment + grad
    master_next = master - rate * (grad + MOMENTUM * moment_next)
    average_next = average + (master_next - average) / (STEP + 1)
    return (master_next, moment_next, average_next, master_next.astype(jnp.bfloat16))


def shards(
    token_ids,
    segments,
    routes,
    positions,
    targets,
    teacher_ids,
    teacher_probs,
    attention,
    attention_moment,
    attention_average,
    expert_in,
    expert_in_moment,
    expert_in_average,
    expert_out,
    expert_out_moment,
    expert_out_average,
    embedding,
    embedding_moment,
    embedding_average,
    small_params,
    small_moment,
    small_average,
):
    members = lax.axis_size("expert")
    replicas = lax.axis_size("dp")
    my_index = lax.axis_index("expert")
    length = segments.shape[1]
    local_rows = segments.shape[0] * length
    width = attention.shape[2]
    local_experts = expert_in.shape[0]
    experts = local_experts * members
    vocab_rows = embedding.shape[0]
    capacity = max(2, 3 * local_rows * TOP // (2 * experts))
    loss_local = positions.shape[0]
    loss_count = loss_local * members * replicas
    scaling = HEAD ** (-0.5)
    highest_precision = lax.Precision.HIGHEST
    share = width // replicas
    chunk = attention.shape[0] * share // members
    small_rows = small_params.size // width + 1
    small_flat = jnp.pad(
        small_params.reshape(-1), (0, small_rows * width - small_params.size)
    ).reshape(small_rows, width)
    dense_part = lax.dynamic_slice_in_dim(
        attention.reshape(attention.shape[0] * share, width), my_index * chunk, chunk, 0
    )
    in_low, out_low, table_low = (
        lax.all_gather(expert_in.astype(jnp.bfloat16), "dp", axis=1, tiled=True),
        lax.all_gather(expert_out.astype(jnp.bfloat16), "dp", axis=1, tiled=True),
        lax.all_gather(embedding.astype(jnp.bfloat16), "dp", axis=1, tiled=True),
    )
    core = lax.axis_index("dp") & 1
    level = lax.axis_index("dp") >> 1
    levels = replicas // 2

    def by_core(value, axis):
        other = dp_swap(value, 1, replicas)
        first = jnp.where(core == 0, value, other)
        return jnp.stack([first, jnp.where(core == 0, other, value)], axis=axis)

    group_ids = token_ids.reshape(-1)
    own_routes = lax.dynamic_slice_in_dim(
        routes.reshape(members * local_rows, TOP), my_index * local_rows, local_rows, 0
    )
    target_local = targets - my_index * vocab_rows
    teacher_local = teacher_ids - my_index * vocab_rows
    taken = label_weights(
        jnp.concatenate([teacher_local, target_local[:, None]], axis=1),
        jnp.concatenate([teacher_probs, jnp.ones_like(teacher_probs[:, :1])], axis=1),
        vocab_rows,
    )
    rows_parts = shared(embedding.astype(jnp.bfloat16), members)
    id_rows = -(-2 * group_ids.shape[0] // width)
    digits = jnp.concatenate([group_ids >> 8, group_ids & 255])
    digits = jnp.pad(digits, (0, id_rows * width - digits.shape[0])).reshape(id_rows, width)
    dense_part = jnp.concatenate([dense_part, small_flat], axis=0).astype(jnp.bfloat16)
    dense_part = jnp.concatenate([dense_part, digits.astype(jnp.bfloat16)], axis=0)
    dense_part, rows_parts[1] = lax.optimization_barrier((dense_part, rows_parts[1]))
    rows_parts[-1], taken = lax.optimization_barrier((rows_parts[-1], taken))
    dense_part = in_order([dp_swap(dense_part, 2 * k, replicas) for k in range(levels)], level)
    others = by_core(dense_part[:, chunk:], 1).reshape(replicas, small_rows + id_rows, width)
    small_low, digits = others[:, :small_rows], others[:, small_rows:].reshape(replicas, -1)
    digits = digits[:, : 2 * group_ids.shape[0]].astype(jnp.int32)
    digits = digits.reshape(replicas, 2, members, local_rows)
    all_ids = digits[:, 0] * 256 + digits[:, 1]
    column_ids = lax.dynamic_index_in_dim(all_ids, my_index, 1, keepdims=False).reshape(-1)
    small_low = small_low.reshape(replicas, small_rows * width)
    small_low = small_low[:, : small_params.size].reshape(replicas, small_params.shape[0], share)
    small_low = small_low.transpose(1, 0, 2).reshape(small_params.shape[0], width)
    gain_rows = small_low[:3].astype(jnp.float32)
    router = small_low[3:].astype(jnp.float32)
    rows_parts[-1], dense_part = lax.optimization_barrier(
        (rows_parts[-1], dense_part[:, :chunk])
    )
    rows_table = jnp.concatenate(rows_parts, axis=0)
    places = partner_of(my_index, column_ids // vocab_rows, members) * vocab_rows
    places = places + column_ids % vocab_rows
    stream_parts = jnp.take(rows_table, places, axis=0, mode="clip")
    dense_parts = shared(dense_part, members)
    stream_parts, dense_parts = lax.optimization_barrier((stream_parts, dense_parts))
    dense_low = by_core(in_order(dense_parts, my_index), 2)
    dense_low = (
        dense_low.reshape(members, replicas, chunk, width)
        .transpose(1, 0, 2, 3)
        .reshape(replicas, attention.shape[0], share, width)
        .transpose(1, 0, 2, 3)
        .reshape(attention.shape[0], width, width)
    )
    stream = lax.all_to_all(
        stream_parts, "dp", split_axis=0, concat_axis=1, tiled=True
    ).astype(jnp.float32)
    token_rows = [
        lax.dynamic_index_in_dim(
            all_ids, partner_of(my_index, k, members), 1, keepdims=False
        ).reshape(-1)
        - my_index * vocab_rows
        for k in range(members)
    ]
    half = members // 2
    early_lists = late_lists = None
    if takes_kernel(half, replicas * local_rows, share):
        early_lists = all_lists(token_rows[:half], vocab_rows)
        late_lists = all_lists(token_rows[half:], vocab_rows)
        stream, early_lists, late_lists = lax.optimization_barrier(
            (stream, early_lists, late_lists)
        )
    normal_one, factor_one = normal_parts(stream)
    attn_in = (normal_one * gain_rows[0]).astype(jnp.bfloat16)
    projected = jnp.einsum(
        "td,jde->jte", attn_in, dense_low[:3], preferred_element_type=jnp.float32
    ).astype(jnp.bfloat16)
    seg_ids = segments.reshape(-1)

    mixed = attend(projected, seg_ids, local_rows // length, scaling)
    hidden_one = stream + jnp.dot(mixed, dense_low[3], preferred_element_type=jnp.float32)
    normal_two, factor_two = normal_parts(hidden_one)
    moe_in = (normal_two * gain_rows[1]).astype(jnp.bfloat16)
    moe_float = moe_in.astype(jnp.float32)
    router_logits = jnp.dot(moe_float, router.T, precision=highest_precision)
    expert_ids = jnp.arange(experts, dtype=jnp.int32)
    route_hits = (own_routes[:, :, None] == expert_ids[None, None, :]).astype(jnp.float32)
    chosen = jnp.sum(router_logits[:, None, :] * route_hits, axis=2)
    gating = jnp.exp(chosen - jnp.max(chosen, axis=1, keepdims=True))
    gating = gating / jnp.sum(gating, axis=1, keepdims=True)
    slots = slot_table(own_routes, experts)
    block = local_experts * capacity
    landing = partner_of(my_index, own_routes // local_experts, members) * block
    landing = landing + own_routes % local_experts * capacity + slots
    landing_iota = jnp.arange(members * block, dtype=jnp.int32)
    picks = [
        (landing[:, j][:, None] == landing_iota[None, :]).astype(jnp.bfloat16) for j in range(TOP)
    ]
    any_pick = sum(picks)

    def exchanged(rows):
        parts = rows.reshape(members, block, rows.shape[1])
        return jnp.stack([swap(parts[k], k, members) for k in range(members)])

    outgoing = jnp.einsum("tr,td->rd", any_pick, moe_in, preferred_element_type=jnp.float32)
    arrived = exchanged(outgoing.astype(jnp.bfloat16))
    arrived = (
        arrived.reshape(members, local_experts, capacity, width)
        .transpose(1, 0, 2, 3)
        .reshape(local_experts, members * capacity, width)
    )

    def sent_back(rows):
        rows = rows.reshape(local_experts, members, capacity, width).transpose(1, 0, 2, 3)
        return exchanged(rows.reshape(members * block, width)).reshape(members * block, width)

    expert_hidden = jnp.einsum("ecd,edf->ecf", arrived, in_low, preferred_element_type=jnp.float32)
    activated = jax.nn.gelu(expert_hidden, approximate=True).astype(jnp.bfloat16)
    expert_result = jnp.einsum(
        "ecf,efd->ecd", activated, out_low, preferred_element_type=jnp.float32
    ).astype(jnp.bfloat16)
    returned = sent_back(expert_result)
    picked = [jnp.dot(pick, returned, preferred_element_type=jnp.float32) for pick in picks]
    hidden_two = hidden_one + sum(gating[:, j][:, None] * picked[j] for j in range(TOP))
    normal_three, factor_three = normal_parts(hidden_two)
    final = (normal_three * gain_rows[2]).astype(jnp.bfloat16)
    place_hits = positions[:, None] == jnp.arange(local_rows, dtype=jnp.int32)[None, :]
    final_rows = jnp.dot(
        place_hits.astype(jnp.bfloat16), final, preferred_element_type=jnp.float32
    ).astype(jnp.bfloat16)
    group_final = lax.all_gather(final_rows, "expert", axis=0, tiled=True)
    logits = jnp.einsum("gd,vd->gv", group_final, table_low, preferred_element_type=jnp.float32)
    taught = jnp.sum(taken * logits, axis=1)
    local_max = jnp.max(logits, axis=1)
    local_total = jnp.sum(jnp.exp(logits - local_max[:, None]), axis=1)
    stats = lax.all_gather(jnp.stack([local_max, local_total, taught]), "expert")
    highest = jnp.max(stats[:, 0], axis=0)
    totals = jnp.sum(stats[:, 1] * jnp.exp(stats[:, 0] - highest[None]), axis=0)
    picked_sum = jnp.sum(stats[:, 2], axis=0)
    log_total = highest + jnp.log(totals)
    entropy = jnp.sum(teacher_probs * jnp.log(teacher_probs), axis=1)
    terms = 2.0 * log_total - picked_sum + entropy
    loss_part = (
        jnp.sum(lax.dynamic_slice_in_dim(terms, my_index * loss_local, loss_local, 0)) / loss_count
    )
    soft = jnp.exp(logits - log_total[:, None])
    logit_grad = ((2.0 * soft - taken) / loss_count).astype(jnp.bfloat16)
    embed_head = jnp.einsum(
        "gv,gd->vd", logit_grad, group_final, preferred_element_type=jnp.float32
    ).astype(jnp.bfloat16)
    embed_head, head_grad = lax.optimization_barrier((embed_head, logit_grad))
    embed_sum = lax.psum_scatter(embed_head, "dp", scatter_dimension=1, tiled=True)
    final_parts = jnp.dot(head_grad, table_low, preferred_element_type=jnp.float32)
    final_grad = sum(
        swap(
            lax.dynamic_slice_in_dim(
                final_parts, partner_of(my_index, k, members) * loss_local, loss_local, 0
            ),
            k,
            members,
        )
        for k in range(members)
    )
    final_full = jnp.dot(
        place_hits.astype(jnp.float32).T, final_grad, precision=highest_precision
    )
    grad_two, gain_three = norm_backward(normal_three, factor_three, gain_rows[2], final_full)
    gate_grad = jnp.stack([jnp.sum(grad_two * part, axis=1) for part in picked], axis=1)
    chosen_grad = gating * (gate_grad - jnp.sum(gating * gate_grad, axis=1, keepdims=True))
    route_grad = jnp.sum(chosen_grad[:, :, None] * route_hits, axis=1)
    router_grad = jnp.dot(route_grad.T, moe_float, precision=highest_precision)
    moe_grad = jnp.dot(route_grad, router, precision=highest_precision)
    outgoing_grad = sum(
        jnp.einsum(
            "tr,td->rd",
            picks[j],
            (gating[:, j][:, None] * grad_two).astype(jnp.bfloat16),
            preferred_element_type=jnp.float32,
        )
        for j in range(TOP)
    ).astype(jnp.bfloat16)
    arrived_grad = (
        exchanged(outgoing_grad)
        .reshape(members, local_experts, capacity, width)
        .transpose(1, 0, 2, 3)
        .reshape(local_experts, members * capacity, width)
    )
    out_grad = jnp.einsum(
        "ecf,ecd->efd", activated, arrived_grad, preferred_element_type=jnp.float32
    )
    activated_grad = jnp.einsum(
        "ecd,efd->ecf", arrived_grad, out_low, preferred_element_type=jnp.float32
    )
    gelu_pull = jax.vjp(lambda inner: jax.nn.gelu(inner, approximate=True), expert_hidden)[1]
    hidden_grad = gelu_pull(activated_grad)[0].astype(jnp.bfloat16)
    in_grad = jnp.einsum("ecd,ecf->edf", arrived, hidden_grad, preferred_element_type=jnp.float32)
    rows_grad = jnp.einsum("ecf,edf->ecd", hidden_grad, in_low, preferred_element_type=jnp.float32)
    back_rows = sent_back(rows_grad.astype(jnp.bfloat16))
    back_rows, out_grad, in_grad, embed_sum = lax.optimization_barrier(
        (back_rows, out_grad.astype(jnp.bfloat16), in_grad.astype(jnp.bfloat16), embed_sum)
    )
    out_sum = lax.psum_scatter(out_grad, "dp", scatter_dimension=1, tiled=True)
    in_sum = lax.psum_scatter(in_grad, "dp", scatter_dimension=1, tiled=True)
    moe_grad = moe_grad + jnp.dot(any_pick, back_rows, preferred_element_type=jnp.float32)
    grad_part, gain_two = norm_backward(normal_two, factor_two, gain_rows[1], moe_grad)
    grad_one = grad_two + grad_part
    attn_grad = grad_one.astype(jnp.bfloat16)
    out_weight_grad = jnp.einsum("tc,td->cd", mixed, attn_grad, preferred_element_type=jnp.float32)
    mixed_grad = jnp.einsum(
        "td,cd->tc", attn_grad, dense_low[3], preferred_element_type=jnp.float32
    )
    mixed_grad = mixed_grad.astype(jnp.bfloat16)

    projected_grad = attend_back(
        projected, mixed_grad, seg_ids, local_rows // length, scaling
    ).astype(jnp.bfloat16)
    qkv_grad = jnp.einsum(
        "td,jte->jde", attn_in, projected_grad, preferred_element_type=jnp.float32
    )
    attn_in_grad = jnp.einsum(
        "jte,jde->td", projected_grad, dense_low[:3], preferred_element_type=jnp.float32
    )
    grad_part, gain_one = norm_backward(normal_one, factor_one, gain_rows[0], attn_in_grad)
    stream_grad = (grad_one + grad_part).astype(jnp.bfloat16)
    attention_grad = jnp.concatenate([qkv_grad, out_weight_grad[None]], axis=0)
    small_grad = jnp.concatenate([jnp.stack([gain_one, gain_two, gain_three]), router_grad], axis=0)
    dense_grads = (
        attention_grad.reshape(attention.shape[0], replicas, share, width)
        .transpose(1, 0, 2, 3)
        .reshape(replicas, members, chunk, width)
        .astype(jnp.bfloat16)
    )
    stream_grad, dense_grads = lax.optimization_barrier((stream_grad, dense_grads))
    column_grad = lax.all_to_all(stream_grad, "dp", split_axis=1, concat_axis=0, tiled=True)
    column_grads = shared(column_grad.T, members)
    small_grads = small_grad.reshape(-1, replicas, share).transpose(1, 0, 2).reshape(replicas, -1)
    small_grads = jnp.concatenate(
        [
            small_grads,
            jnp.full((replicas, 1), loss_part),
            jnp.zeros((replicas, small_rows * width - small_params.size - 1), jnp.float32),
        ],
        axis=1,
    ).reshape(replicas, small_rows, width)

    def spread(values):
        return jnp.concatenate([part.astype(jnp.bfloat16) for part in in_thirds(values)], axis=1)

    def joined(values):
        parts = values.reshape(values.shape[0], -1, small_rows, width).astype(jnp.float32)
        return jnp.sum(parts, axis=1)

    def packed(dense, small):
        return jnp.concatenate([dense.astype(jnp.bfloat16), spread(small)], axis=1)

    def of_core(values, which):
        values = values.reshape((levels, 2) + values.shape[1:])
        return lax.dynamic_index_in_dim(values, which, 1, keepdims=False)

    dense_sum = of_core(dense_grads, core).astype(jnp.float32) + dp_swap(
        of_core(dense_grads, 1 - core), 1, replicas
    ).astype(jnp.float32)
    small_sum = of_core(small_grads, core) + joined(
        dp_swap(spread(of_core(small_grads, 1 - core)), 1, replicas)
    )
    received = [
        swap(
            packed(
                lax.dynamic_index_in_dim(
                    dense_sum, partner_of(my_index, k, members), 1, keepdims=False
                ),
                small_sum,
            ),
            k,
            members,
        )
        for k in range(members)
    ]
    column_grads[1], out_sum = lax.optimization_barrier((column_grads[1], out_sum))
    third_out = nesterov_update(
        expert_out,
        expert_out_moment,
        expert_out_average,
        out_sum.astype(jnp.float32),
        RATE_TABLE[2] * loss_count**0.5,
    )
    stream_sum = add_rows(token_rows[:half], early_lists, column_grads[:half], vocab_rows, None)
    received, stream_sum = lax.optimization_barrier((received, stream_sum))
    dense_sum = sum(part[:, :chunk].astype(jnp.float32) for part in received)
    small_sum = sum(joined(part[:, chunk:]) for part in received)
    message = packed(dense_sum, small_sum)
    summed = lax.dynamic_index_in_dim(dense_sum, level, 0, keepdims=False)
    small_sum = lax.dynamic_index_in_dim(small_sum, level, 0)
    for k in range(1, levels):
        part = dp_swap(lax.dynamic_index_in_dim(message, level ^ k, 0), 2 * k, replicas)
        summed = summed + part[0, :chunk].astype(jnp.float32)
        small_sum = small_sum + joined(part[:, chunk:])
    small_sum = small_sum.reshape(-1)
    column_grads[-1], third_out, summed = lax.optimization_barrier(
        (column_grads[-1], third_out, summed)
    )
    stream_sum = add_rows(token_rows[half:], late_lists, column_grads[half:], vocab_rows, stream_sum)
    embed_sum = embed_sum.astype(jnp.float32) + stream_sum.T
    loss_value = small_sum[small_params.size]
    small_sum = small_sum[: small_params.size].reshape(small_params.shape[0], share)
    attention_sum = in_order(shared(summed, members), my_index)
    attention_sum = attention_sum.reshape(attention.shape[0], share, width)
    rate_base = loss_count**0.5
    first_out = nesterov_update(
        attention, attention_moment, attention_average, attention_sum, RATE_TABLE[0] * rate_base
    )
    fourth_out = nesterov_update(
        embedding, embedding_moment, embedding_average, embed_sum, RATE_TABLE[3] * rate_base
    )
    fifth_out = nesterov_update(
        small_params, small_moment, small_average, small_sum, RATE_TABLE[4] * rate_base
    )
    first_out, fourth_out, fifth_out, in_sum = lax.optimization_barrier(
        (first_out, fourth_out, fifth_out, in_sum)
    )
    second_out = nesterov_update(
        expert_in, expert_in_moment, expert_in_average, in_sum.astype(jnp.float32), RATE_TABLE[1] * rate_base
    )
    return (loss_value,) + first_out + second_out + third_out + fourth_out + fifth_out


def solution(mesh):
    return jax.shard_map(
        shards,
        mesh=mesh,
        in_specs=(
            P("dp", None),
            P(("dp", "expert"), None),
            P("dp", None, None),
            P(("dp", "expert")),
            P("dp"),
            P("dp", None),
            P("dp", None),
            P(None, "dp", None),
            P(None, "dp", None),
            P(None, "dp", None),
            P("expert", "dp", None),
            P("expert", "dp", None),
            P("expert", "dp", None),
            P("expert", "dp", None),
            P("expert", "dp", None),
            P("expert", "dp", None),
            P("expert", "dp"),
            P("expert", "dp"),
            P("expert", "dp"),
            P(None, "dp"),
            P(None, "dp"),
            P(None, "dp"),
        ),
        out_specs=(
            P(),
            P(None, "dp", None),
            P(None, "dp", None),
            P(None, "dp", None),
            P(None, "dp", None),
            P("expert", "dp", None),
            P("expert", "dp", None),
            P("expert", "dp", None),
            P("expert", "dp", None),
            P("expert", "dp", None),
            P("expert", "dp", None),
            P("expert", "dp", None),
            P("expert", "dp", None),
            P("expert", "dp"),
            P("expert", "dp"),
            P("expert", "dp"),
            P("expert", "dp"),
            P(None, "dp"),
            P(None, "dp"),
            P(None, "dp"),
            P(None, "dp"),
        ),
        check_vma=False,
    )
```
